32 devices in a mesh: fsdp: 8 (over y, x, core), tp: 4 (over z).
Axes of the slice: x: 2, y: 2, z: 4, core: 2. Of those that a mesh axis runs over, the one named last changes fastest.
Arguments:
- tokens: bfloat16 [2, 2048, 2048], P(None, 'fsdp', 'tp'), may hold values from -6 to 6
- out_grad: bfloat16 [2, 2048, 2048], P(None, 'fsdp', 'tp'), may hold values from -6 to 6
- segment_ids: int32 [2, 2048], P(None, 'fsdp'), may hold values from 0 to 3, as said below
- positions: int32 [2, 2048], P(None, 'fsdp'), may hold values from 0 to 1023, as said below
- attn_norm: bfloat16 [2048], P('fsdp'), may hold values from 0.25 to 1.75
- w_query: bfloat16 [2048, 2048], P('fsdp', 'tp'), may hold values from -0.125 to 0.125
- key_projection_weight: bfloat16 [2048, 256], P('fsdp', 'tp'), may hold values from -0.125 to 0.125
- value_projection_weight: bfloat16 [2048, 256], P('fsdp', 'tp'), may hold values from -0.125 to 0.125
- w_out: bfloat16 [2048, 2048], P('tp', 'fsdp'), may hold values from -1 to 1
- mlp_norm: bfloat16 [2048], P('fsdp'), may hold values from 0.25 to 1.75
- w_gate: bfloat16 [2048, 5632], P('fsdp', 'tp'), may hold values from -0.125 to 0.125
- w_up: bfloat16 [2048, 5632], P('fsdp', 'tp'), may hold values from -0.125 to 0.125
- w_down: bfloat16 [5632, 2048], P('tp', 'fsdp'), may hold values from -0.078125 to 0.078125
Outputs:
- layer_out: bfloat16 [2, 2048, 2048], P(None, 'fsdp', 'tp')
- input_grad: float32 [2, 2048, 2048], P(None, 'fsdp', 'tp')
- grad_attn_norm: float32 [2048], P('fsdp')
- grad_query: float32 [2048, 2048], P('fsdp', 'tp')
- grad_key: float32 [2048, 256], P('fsdp', 'tp')
- grad_value: float32 [2048, 256], P('fsdp', 'tp')
- grad_out: float32 [2048, 2048], P('tp', 'fsdp')
- grad_mlp_norm: float32 [2048], P('fsdp')
- grad_gate: float32 [2048, 5632], P('fsdp', 'tp')
- grad_up: float32 [2048, 5632], P('fsdp', 'tp')
- grad_down: float32 [5632, 2048], P('tp', 'fsdp')
The draws below stay inside these ranges and needn't reach their ends.
Inputs may be any that keep to these rules, and one draw needn't show every extreme that they name: `segment_ids`: within each sequence of 2048 tokens, taken in its own order, the ids run 0, 1, 2, 3 in order, each a contiguous run of 1 token or more; one run in each sequence is exactly 1024 tokens long. `positions`: each token's offset, in its sequence's order, from the first token of its run of equal segment_ids.
All inputs are finite; a program needn't handle non-finite values.
Results may differ from the reference program's by a relative error of at most 0.014.
Values may be sent and summed in bfloat16 or wider, within the bound.
No kernel may reach another device: no remote copies, remote signals or barrier semaphores. Data moves between devices by JAX's collectives and lax.ppermute only.
A program may use at most 256 MiB of HBM per device.

```python
import jax
import jax.numpy as jnp
from jax import lax

MODEL_WIDTH = 2048
GATED_HIDDEN = 5632
QUERY_HEADS = 32
KEY_VALUE_HEADS = 4
HEAD_SIZE = 64
SEQUENCE_LENGTH = 2048
MB = 2
TOK_DEV = 256
DOC_MAX = 1024
TOKENS = 2048


def document_layout(key):
    seq_count = TOKENS // SEQUENCE_LENGTH
    part_count = SEQUENCE_LENGTH // TOK_DEV
    sequences = MB * seq_count
    layout_key = jax.random.fold_in(key, 11)
    first_key, second_key, third_key = jax.random.split(layout_key, 3)
    half_span = DOC_MAX // 2
    first_cut = jax.random.randint(first_key, (sequences,), 1, half_span)
    second_cut = first_cut + jax.random.randint(second_key, (sequences,), 1, half_span)
    short_docs = jnp.stack([first_cut, second_cut - first_cut, DOC_MAX - second_cut], -1).astype(jnp.int32)
    long_slot = jax.random.randint(third_key, (sequences, 1), 0, 4).astype(jnp.int32)
    slot_ids = jnp.arange(4, dtype=jnp.int32)[None, :]
    picked = jnp.clip(slot_ids - (slot_ids > long_slot).astype(jnp.int32), 0, 2)
    lengths = jnp.where(slot_ids == long_slot, DOC_MAX, jnp.take_along_axis(short_docs, picked, 1)).astype(jnp.int32)
    starts = jnp.cumsum(lengths, 1) - lengths
    token_ids = jnp.arange(SEQUENCE_LENGTH, dtype=jnp.int32)
    segment = jnp.sum((token_ids[None, :, None] >= starts[:, None, 1:]).astype(jnp.int32), -1)
    offsets = jnp.take_along_axis(starts, segment, 1)
    position = token_ids[None, :] - offsets

    def placed(values):
        shaped = values.reshape(MB, seq_count, part_count, TOK_DEV)
        return jnp.swapaxes(shaped, 1, 2).reshape(MB, TOKENS).astype(jnp.int32)
    return (placed(segment), placed(position))


def draw_segment_ids(key, part):
    return document_layout(key)[0]


def draw_positions(key, part):
    return document_layout(key)[1]


def steps_of(stream_key, dims, cuts, least, top_value):
    def one(axis_at, blocks):
        steps = jax.random.uniform(jax.random.fold_in(jax.random.fold_in(stream_key, 6), axis_at), (blocks,), jnp.float32, least / len(cuts), top_value / len(cuts))
        return jnp.repeat(jnp.exp(steps), dims[axis_at] // blocks).reshape((-1,) + (1,) * (len(dims) - axis_at - 1))

    level = one(*cuts[0])
    for cut in cuts[1:]:
        level = level * one(*cut)
    return level


def bell_draw(stream_key, dims, width, reach, shards=(), kind=jnp.bfloat16):
    level = steps_of(stream_key, dims, shards, -0.22, 0.18) if shards else 1.0
    values = jax.random.normal(stream_key, dims, jnp.float32) * width * level
    return jnp.minimum(jnp.maximum(values, -reach), reach).astype(kind)


def setup_inputs(seed: int = 0) -> dict:
    keys = jax.random.split(jax.random.key(seed), 14)
    return {
        "tokens": bell_draw(keys[0], (MB, TOKENS, MODEL_WIDTH), 1.0, 6.0, ((1, 8), (2, 4))),
        "out_grad": bell_draw(keys[1], (MB, TOKENS, MODEL_WIDTH), 1.0, 6.0, ((1, 8), (2, 4))),
        "segment_ids": draw_segment_ids(jax.random.fold_in(keys[13], 71), 0),
        "positions": draw_positions(jax.random.fold_in(keys[13], 71), 0),
        "attn_norm": jnp.clip(1.0 + 0.15 * jax.random.normal(keys[4], (MODEL_WIDTH,), jnp.float32), 0.25, 1.75).astype(jnp.bfloat16),
        "w_query": bell_draw(keys[5], (MODEL_WIDTH, QUERY_HEADS * HEAD_SIZE), MODEL_WIDTH ** -0.5, 0.125, ((0, 8), (1, 4))),
        "key_projection_weight": bell_draw(keys[6], (MODEL_WIDTH, KEY_VALUE_HEADS * HEAD_SIZE), MODEL_WIDTH ** -0.5, 0.125, ((0, 8), (1, 4))),
        "value_projection_weight": bell_draw(keys[7], (MODEL_WIDTH, KEY_VALUE_HEADS * HEAD_SIZE), MODEL_WIDTH ** -0.5, 0.125, ((0, 8), (1, 4))),
        "w_out": bell_draw(keys[8], (QUERY_HEADS * HEAD_SIZE, MODEL_WIDTH), (max(QUERY_HEADS * HEAD_SIZE // 64, 2)) ** -0.5, 1.0, ((0, 4), (1, 8))),
        "mlp_norm": jnp.clip(1.0 + 0.15 * jax.random.normal(keys[9], (MODEL_WIDTH,), jnp.float32), 0.25, 1.75).astype(jnp.bfloat16),
        "w_gate": bell_draw(keys[10], (MODEL_WIDTH, GATED_HIDDEN), MODEL_WIDTH ** -0.5, 0.125, ((0, 8), (1, 4))),
        "w_up": bell_draw(keys[11], (MODEL_WIDTH, GATED_HIDDEN), MODEL_WIDTH ** -0.5, 0.125, ((0, 8), (1, 4))),
        "w_down": bell_draw(keys[12], (GATED_HIDDEN, MODEL_WIDTH), GATED_HIDDEN ** -0.5, 0.078125, ((0, 4), (1, 8))),
    }


NORM_EPSILON = 1e-05
ROPE_BASE = 10000.0
MASKED_SCORE = -1e+30

def to_sequences(values):
    rest = values.shape[2:]
    part_count = SEQUENCE_LENGTH // TOK_DEV
    seq_count = TOKENS // SEQUENCE_LENGTH
    shaped = values.reshape((MB, part_count, seq_count, TOK_DEV) + rest)
    return jnp.swapaxes(shaped, 1, 2).reshape((MB * seq_count, SEQUENCE_LENGTH) + rest)

def from_sequences(values):
    rest = values.shape[2:]
    part_count = SEQUENCE_LENGTH // TOK_DEV
    seq_count = TOKENS // SEQUENCE_LENGTH
    shaped = values.reshape((MB, seq_count, part_count, TOK_DEV) + rest)
    return jnp.swapaxes(shaped, 1, 2).reshape((MB, TOKENS) + rest)

def rope_tables(offsets, head_width):
    half_width = head_width // 2
    inverse = ROPE_BASE ** (-(jnp.arange(half_width, dtype=jnp.float32) * 2.0 / head_width))
    angles = offsets.astype(jnp.float32)[:, None] * inverse[None, :]
    cosine_table = jnp.concatenate([jnp.cos(angles), jnp.cos(angles)], -1)
    sine_lookup = jnp.concatenate([jnp.sin(angles), jnp.sin(angles)], -1)
    return (cosine_table, sine_lookup)

def apply_rotary(vectors, cosine_table, sine_lookup):
    half_width = vectors.shape[-1] // 2
    turned = jnp.concatenate([-vectors[..., half_width:], vectors[..., :half_width]], -1)
    return vectors * cosine_table[:, None, :] + turned * sine_lookup[:, None, :]

def reverse_rotary(cotangent, cosine_table, sine_lookup):
    half_width = cotangent.shape[-1] // 2
    scaled = cotangent * sine_lookup[:, None, :]
    return cotangent * cosine_table[:, None, :] + jnp.concatenate([scaled[..., half_width:], -scaled[..., :half_width]], -1)

def group_scores(query_rotated, key_rows, score_scale):
    return jnp.einsum('lhd,md->hlm', query_rotated.astype(jnp.float32), key_rows.astype(jnp.float32)) * score_scale

def attend_forward(query_rotated, key_rows, value_rows, allowed, score_scale):
    scores = group_scores(query_rotated, key_rows, score_scale)
    row_max = lax.optimization_barrier(jnp.max(jnp.where(allowed, scores, MASKED_SCORE), -1))
    row_sum = lax.optimization_barrier(jnp.sum(jnp.where(allowed, jnp.exp(scores - row_max[..., None]), 0.0), -1))
    log_total = row_max + jnp.log(row_sum)
    prob_round = jnp.where(allowed, jnp.exp(scores - log_total[..., None]), 0.0).astype(jnp.bfloat16)
    heads_sum = jnp.einsum('hlm,md->lhd', prob_round.astype(jnp.float32), value_rows.astype(jnp.float32))
    return (heads_sum.astype(jnp.bfloat16), log_total)

def attend_backward(query_rotated, key_rows, value_rows, log_total, heads_low, grad_low, allowed, score_scale):
    scores = group_scores(query_rotated, key_rows, score_scale)
    prob_exact = jnp.where(allowed, jnp.exp(scores - log_total[..., None]), 0.0)
    prob_round = prob_exact.astype(jnp.bfloat16)
    grad_values = jnp.einsum('hlm,lhd->md', prob_round.astype(jnp.float32), grad_low.astype(jnp.float32))
    grad_probs = jnp.einsum('lhd,md->hlm', grad_low.astype(jnp.float32), value_rows.astype(jnp.float32))
    delta = jnp.einsum('lhd,lhd->hl', grad_low.astype(jnp.float32), heads_low.astype(jnp.float32))
    grad_scores = (prob_exact * (grad_probs - delta[..., None]) * score_scale).astype(jnp.bfloat16)
    grad_query = jnp.einsum('hlm,md->lhd', grad_scores.astype(jnp.float32), key_rows.astype(jnp.float32))
    grad_keys = jnp.einsum('hlm,lhd->md', grad_scores.astype(jnp.float32), query_rotated.astype(jnp.float32))
    return (grad_query, grad_keys, grad_values)

def reference(tokens, out_grad, segment_ids, positions, attn_norm, w_query, key_projection_weight, value_projection_weight, w_out, mlp_norm, w_gate, w_up, w_down):
    heads_per_group = QUERY_HEADS // KEY_VALUE_HEADS
    score_scale = HEAD_SIZE ** (-0.5)
    gain_one = attn_norm.astype(jnp.float32)
    gain_two = mlp_norm.astype(jnp.float32)
    token_ids = jnp.arange(SEQUENCE_LENGTH, dtype=jnp.int32)

    def layer_step(carry, inputs):
        acc_norm_one, acc_query, acc_key, acc_value, acc_out, acc_norm_two, acc_gate, acc_up, acc_down = carry
        block_in, block_grad, block_segments, block_offsets = inputs
        input_float = block_in.astype(jnp.float32)
        scale_one = lax.rsqrt(lax.optimization_barrier(jnp.mean(input_float * input_float, -1, keepdims=True)) + NORM_EPSILON)
        normed_one = (input_float * scale_one * gain_one).astype(jnp.bfloat16)
        query = jnp.dot(normed_one, w_query, preferred_element_type=jnp.float32)
        key_projected = jnp.dot(normed_one, key_projection_weight, preferred_element_type=jnp.float32)
        value_projected = jnp.dot(normed_one, value_projection_weight, preferred_element_type=jnp.float32)
        cosine_table, sine_lookup = rope_tables(block_offsets, HEAD_SIZE)
        query_rotated = apply_rotary(query.reshape(SEQUENCE_LENGTH, QUERY_HEADS, HEAD_SIZE), cosine_table, sine_lookup).astype(jnp.bfloat16)
        key_rotated = apply_rotary(key_projected.reshape(SEQUENCE_LENGTH, KEY_VALUE_HEADS, HEAD_SIZE), cosine_table, sine_lookup).astype(jnp.bfloat16)
        value_narrow = value_projected.astype(jnp.bfloat16).reshape(SEQUENCE_LENGTH, KEY_VALUE_HEADS, HEAD_SIZE)
        allowed = ((block_segments[:, None] == block_segments[None, :]) & (token_ids[None, :] <= token_ids[:, None]))[None]
        query_by_group = query_rotated.reshape(SEQUENCE_LENGTH, KEY_VALUE_HEADS, heads_per_group, HEAD_SIZE).transpose(1, 0, 2, 3)
        key_groups = key_rotated.transpose(1, 0, 2)
        value_groups = value_narrow.transpose(1, 0, 2)

        def forward_group(operands):
            return attend_forward(operands[0], operands[1], operands[2], allowed, score_scale)
        out_groups, log_totals = lax.map(forward_group, (query_by_group, key_groups, value_groups))
        heads_out = out_groups.transpose(1, 0, 2, 3).reshape(SEQUENCE_LENGTH, QUERY_HEADS * HEAD_SIZE)
        middle = input_float + jnp.dot(heads_out, w_out, preferred_element_type=jnp.float32)
        scale_two = lax.rsqrt(lax.optimization_barrier(jnp.mean(middle * middle, -1, keepdims=True)) + NORM_EPSILON)
        normed_two = (middle * scale_two * gain_two).astype(jnp.bfloat16)
        gate = jnp.dot(normed_two, w_gate, preferred_element_type=jnp.float32)
        up_proj = jnp.dot(normed_two, w_up, preferred_element_type=jnp.float32)
        sigmoid_gate = jax.nn.sigmoid(gate)
        activated = (gate * sigmoid_gate * up_proj).astype(jnp.bfloat16)
        layer_out = (middle + jnp.dot(activated, w_down, preferred_element_type=jnp.float32)).astype(jnp.bfloat16)
        grad_float = block_grad.astype(jnp.float32)
        acc_down = acc_down + jnp.dot(activated.T, block_grad, preferred_element_type=jnp.float32)
        grad_act = jnp.dot(block_grad, w_down.T, preferred_element_type=jnp.float32)
        grad_gate_low = (grad_act * up_proj * sigmoid_gate * (1.0 + gate * (1.0 - sigmoid_gate))).astype(jnp.bfloat16)
        grad_up_low = (grad_act * gate * sigmoid_gate).astype(jnp.bfloat16)
        acc_gate = acc_gate + jnp.dot(normed_two.T, grad_gate_low, preferred_element_type=jnp.float32)
        acc_up = acc_up + jnp.dot(normed_two.T, grad_up_low, preferred_element_type=jnp.float32)
        grad_normed_two = jnp.dot(grad_gate_low, w_gate.T, preferred_element_type=jnp.float32) + jnp.dot(grad_up_low, w_up.T, preferred_element_type=jnp.float32)
        acc_norm_two = acc_norm_two + lax.optimization_barrier(jnp.sum(grad_normed_two * middle * scale_two, 0))
        scaled_two = grad_normed_two * gain_two
        grad_middle = grad_float + scale_two * scaled_two - middle * (scale_two * scale_two * scale_two) * lax.optimization_barrier(jnp.mean(scaled_two * middle, -1, keepdims=True))
        middle_low = grad_middle.astype(jnp.bfloat16)
        acc_out = acc_out + jnp.dot(heads_out.T, middle_low, preferred_element_type=jnp.float32)
        gradient_by_head = jnp.dot(middle_low, w_out.T, preferred_element_type=jnp.float32).astype(jnp.bfloat16)
        gradient_by_group = gradient_by_head.reshape(SEQUENCE_LENGTH, KEY_VALUE_HEADS, heads_per_group, HEAD_SIZE).transpose(1, 0, 2, 3)

        def backward_group(operands):
            return attend_backward(operands[0], operands[1], operands[2], operands[3], operands[4], operands[5], allowed, score_scale)
        query_back, key_backward_pass, value_backward_pass = lax.map(backward_group, (query_by_group, key_groups, value_groups, log_totals, out_groups, gradient_by_group))
        grad_query_low = reverse_rotary(query_back.transpose(1, 0, 2, 3).reshape(SEQUENCE_LENGTH, QUERY_HEADS, HEAD_SIZE), cosine_table, sine_lookup).reshape(SEQUENCE_LENGTH, QUERY_HEADS * HEAD_SIZE).astype(jnp.bfloat16)
        key_gradient_narrow = reverse_rotary(key_backward_pass.transpose(1, 0, 2), cosine_table, sine_lookup).reshape(SEQUENCE_LENGTH, KEY_VALUE_HEADS * HEAD_SIZE).astype(jnp.bfloat16)
        value_gradient_narrow = value_backward_pass.transpose(1, 0, 2).reshape(SEQUENCE_LENGTH, KEY_VALUE_HEADS * HEAD_SIZE).astype(jnp.bfloat16)
        acc_query = acc_query + jnp.dot(normed_one.T, grad_query_low, preferred_element_type=jnp.float32)
        acc_key = acc_key + jnp.dot(normed_one.T, key_gradient_narrow, preferred_element_type=jnp.float32)
        acc_value = acc_value + jnp.dot(normed_one.T, value_gradient_narrow, preferred_element_type=jnp.float32)
        grad_normed_one = jnp.dot(grad_query_low, w_query.T, preferred_element_type=jnp.float32) + jnp.dot(key_gradient_narrow, key_projection_weight.T, preferred_element_type=jnp.float32) + jnp.dot(value_gradient_narrow, value_projection_weight.T, preferred_element_type=jnp.float32)
        acc_norm_one = acc_norm_one + lax.optimization_barrier(jnp.sum(grad_normed_one * input_float * scale_one, 0))
        scaled_one = grad_normed_one * gain_one
        input_grad = grad_middle + scale_one * scaled_one - input_float * (scale_one * scale_one * scale_one) * lax.optimization_barrier(jnp.mean(scaled_one * input_float, -1, keepdims=True))
        new_carry = (acc_norm_one, acc_query, acc_key, acc_value, acc_out, acc_norm_two, acc_gate, acc_up, acc_down)
        return (new_carry, (layer_out, input_grad))
    start_offset = (jnp.zeros((MODEL_WIDTH,), jnp.float32), jnp.zeros((MODEL_WIDTH, QUERY_HEADS * HEAD_SIZE), jnp.float32), jnp.zeros((MODEL_WIDTH, KEY_VALUE_HEADS * HEAD_SIZE), jnp.float32), jnp.zeros((MODEL_WIDTH, KEY_VALUE_HEADS * HEAD_SIZE), jnp.float32), jnp.zeros((QUERY_HEADS * HEAD_SIZE, MODEL_WIDTH), jnp.float32), jnp.zeros((MODEL_WIDTH,), jnp.float32), jnp.zeros((MODEL_WIDTH, GATED_HIDDEN), jnp.float32), jnp.zeros((MODEL_WIDTH, GATED_HIDDEN), jnp.float32), jnp.zeros((GATED_HIDDEN, MODEL_WIDTH), jnp.float32))
    inputs = (to_sequences(tokens), to_sequences(out_grad), to_sequences(segment_ids), to_sequences(positions))
    totals, (outputs, input_grads) = lax.scan(layer_step, start_offset, inputs)
    grad_scale = (MB * TOKENS) ** (-0.5)
    return (from_sequences(outputs), from_sequences(input_grads), totals[0] * grad_scale, totals[1] * grad_scale, totals[2] * grad_scale, totals[3] * grad_scale, totals[4] * grad_scale, totals[5] * grad_scale, totals[6] * grad_scale, totals[7] * grad_scale, totals[8] * grad_scale)
```

```python
import jax
import jax.numpy as jnp
from jax import lax
from jax.sharding import PartitionSpec as P

HEAD_SIZE = 64
SEQUENCE_LENGTH = 2048
DOC_MAX = 1024


NORM_EPSILON = 1e-05
ROPE_BASE = 10000.0
MASKED_SCORE = -1e30
GAIN_COLUMNS = 128

F32 = jnp.float32
BF16 = jnp.bfloat16


def rope_tables(offsets, head_width):
    half_width = head_width // 2
    inverse = ROPE_BASE ** (-(jnp.arange(half_width, dtype=F32) * 2.0 / head_width))
    angles = offsets.astype(F32)[:, None] * inverse[None, :]
    cosine_table = jnp.concatenate([jnp.cos(angles), jnp.cos(angles)], -1)
    sine_lookup = jnp.concatenate([jnp.sin(angles), jnp.sin(angles)], -1)
    return (cosine_table, sine_lookup)


def apply_rotary(vectors, cosine_table, sine_lookup):
    half_width = vectors.shape[-1] // 2
    turned = jnp.concatenate([-vectors[..., half_width:], vectors[..., :half_width]], -1)
    return vectors * cosine_table[:, None, :] + turned * sine_lookup[:, None, :]


def reverse_rotary(cotangent, cosine_table, sine_lookup):
    half_width = cotangent.shape[-1] // 2
    scaled = cotangent * sine_lookup[:, None, :]
    return cotangent * cosine_table[:, None, :] + jnp.concatenate(
        [scaled[..., half_width:], -scaled[..., :half_width]], -1
    )


def dot_nn(left, right):
    return jnp.dot(left, right, preferred_element_type=F32)


def dot_nt(left, right):
    return lax.dot_general(left, right, (((1,), (1,)), ((), ())), preferred_element_type=F32)


def dot_tn(left, right):
    return lax.dot_general(left, right, (((0,), (0,)), ((), ())), preferred_element_type=F32)


def exchange(block, axis, mask):
    return lax.ppermute(block, axis, [(i, i ^ mask) for i in range(lax.axis_size(axis))])


def passed_along(block, axis, distance):
    devices = range(lax.axis_size(axis))
    route = [(i - distance, i) for i in devices if i - distance in devices]
    return lax.ppermute(block, axis, route)


def tp_gather(part):
    size = lax.axis_size("tp")
    index = lax.axis_index("tp")
    held = part[None]
    bit = size // 2
    order = []
    while bit:
        other = exchange(held, "tp", bit)
        mine_first = (index & bit) == 0
        held = jnp.where(
            mine_first, jnp.stack([held, other]), jnp.stack([other, held])
        )
        order.append(bit)
        bit //= 2
    held = held.reshape((2,) * len(order) + part.shape)
    axes = tuple(reversed(range(len(order))))
    held = held.transpose((len(order),) + axes + (len(order) + 1,))
    return held.reshape(part.shape[0], size * part.shape[1])


def tp_scatter_sum(partial):
    size = lax.axis_size("tp")
    index = lax.axis_index("tp")
    rows, full = partial.shape
    held = partial.reshape(rows, size, full // size)
    bit = 1
    slots = size
    while bit < size:
        split = held.reshape(rows, slots // 2, 2, full // size)
        low = (index & bit) == 0
        keep = jnp.where(low, split[:, :, 0], split[:, :, 1])
        send = jnp.where(low, split[:, :, 1], split[:, :, 0]).astype(BF16)
        held = keep + exchange(send, "tp", bit).astype(F32)
        slots //= 2
        bit *= 2
    return held.reshape(rows, full // size)


def queue_gather(part):
    return lax.all_gather(part, "tp", axis=1, tiled=True)


def queue_scatter_sum(partial):
    return lax.psum_scatter(partial.astype(BF16), "tp", scatter_dimension=1, tiled=True)


def owner_block(array, owner, axis):
    width = array.shape[axis] // lax.axis_size("fsdp")
    return lax.dynamic_slice_in_dim(array, owner * width, width, axis)


def owner_sums(block_of):
    size = lax.axis_size("fsdp")
    index = lax.axis_index("fsdp")
    pairs = size // 2
    away = jnp.stack([block_of((index ^ 1) ^ (2 * m)).astype(BF16) for m in range(pairs)])
    other = exchange(away, "fsdp", 1)
    total = None
    for m in reversed(range(pairs)):
        term = block_of(index ^ (2 * m)) + other[m].astype(F32)
        if m:
            term = exchange(term.astype(BF16), "fsdp", 2 * m).astype(F32)
        total = term if total is None else total + term
    return total


def allowed_keys(offsets, row_count, back):
    row = jnp.arange(row_count, dtype=jnp.int32)[:, None] + back * row_count
    first = row - offsets[:, None]
    key = jnp.arange((back + 1) * row_count, dtype=jnp.int32)[None, :]
    return ((key >= first) & (key <= row))[None]


def attend_forward(query_rotated, keys, values, allowed, score_scale):
    scores = (
        jnp.einsum("lhd,md->hlm", query_rotated, keys, preferred_element_type=F32) * score_scale
    )
    scores = jnp.where(allowed, scores, MASKED_SCORE)
    row_max = jnp.max(scores, -1)
    row_sum = jnp.sum(jnp.where(allowed, jnp.exp(scores - row_max[..., None]), 0.0), -1)
    log_total = row_max + jnp.log(row_sum)
    prob_round = jnp.where(allowed, jnp.exp(scores - log_total[..., None]), 0.0).astype(BF16)
    heads = jnp.einsum("hlm,md->lhd", prob_round, values, preferred_element_type=F32)
    return (heads.astype(BF16), log_total)


def attend_backward(
    query_rotated, keys, values, allowed, log_total, heads_low, grad_low, score_scale
):
    delta = jnp.sum(grad_low.astype(F32) * heads_low.astype(F32), -1).T
    scores = (
        jnp.einsum("lhd,md->hlm", query_rotated, keys, preferred_element_type=F32) * score_scale
    )
    prob_exact = jnp.where(allowed, jnp.exp(scores - log_total[..., None]), 0.0)
    prob_round = prob_exact.astype(BF16)
    grad_values = jnp.einsum("hlm,lhd->md", prob_round, grad_low, preferred_element_type=F32)
    grad_probs = jnp.einsum("lhd,md->hlm", grad_low, values, preferred_element_type=F32)
    grad_scores = (prob_exact * (grad_probs - delta[..., None]) * score_scale).astype(BF16)
    grad_query = jnp.einsum("hlm,md->lhd", grad_scores, keys, preferred_element_type=F32)
    grad_keys = jnp.einsum("hlm,lhd->md", grad_scores, query_rotated, preferred_element_type=F32)
    return (grad_query, grad_keys, grad_values)


def shards(
    tokens,
    out_grad,
    segment_ids,
    positions,
    attn_norm,
    w_query,
    key_projection_weight,
    value_projection_weight,
    w_out,
    mlp_norm,
    w_gate,
    w_up,
    w_down,
):
    batch_count, row_count, local_width = tokens.shape
    batches = range(batch_count)
    full_width = local_width * lax.axis_size("tp")
    group_size = SEQUENCE_LENGTH // row_count
    stride = lax.axis_size("fsdp") // group_size
    query_width = w_query.shape[1]
    hidden = w_gate.shape[1]
    head_count = query_width // HEAD_SIZE
    score_scale = HEAD_SIZE ** (-0.5)
    back = min(group_size - 1, -(-(DOC_MAX - 1) // row_count))
    column_start = lax.axis_index("tp") * local_width
    shard_rows = w_query.shape[0]

    gains = jnp.stack([attn_norm, mlp_norm], 1)
    gains = jnp.pad(gains, ((0, 0), (0, GAIN_COLUMNS - 2)))
    first_shard = jnp.concatenate(
        [w_query, key_projection_weight, value_projection_weight, gains], 1
    )
    first_full = lax.all_gather(first_shard, "fsdp", axis=0, tiled=True)
    project_width = query_width + 2 * HEAD_SIZE
    project_weight = first_full[:, :project_width]
    gain_rows = first_full[:, project_width : project_width + 2].astype(F32).T
    gain_one, gain_two = gain_rows[0], gain_rows[1]
    out_weight = lax.all_gather(w_out, "fsdp", axis=1, tiled=True)
    gate_up_weight = lax.all_gather(
        jnp.concatenate([w_gate, w_up], 1), "fsdp", axis=0, tiled=True
    )
    down_weight = lax.all_gather(w_down, "fsdp", axis=1, tiled=True)

    inputs = [tp_gather(tokens[b]).astype(F32) for b in batches]
    scale_one = [
        lax.rsqrt(jnp.mean(x * x, -1, keepdims=True) + NORM_EPSILON) for x in inputs
    ]
    normed_one = jnp.concatenate(
        [(inputs[b] * scale_one[b] * gain_one).astype(BF16) for b in batches], 0
    )
    projected = dot_nn(normed_one, project_weight)
    cosine_table, sine_lookup = rope_tables(positions.reshape(-1), HEAD_SIZE)
    query_rotated = apply_rotary(
        projected[:, :query_width].reshape(-1, head_count, HEAD_SIZE), cosine_table, sine_lookup
    ).astype(BF16)
    key_rotated = apply_rotary(
        projected[:, None, query_width : query_width + HEAD_SIZE], cosine_table, sine_lookup
    )[:, 0].astype(BF16)
    pairs = jnp.concatenate(
        [key_rotated, projected[:, query_width + HEAD_SIZE :].astype(BF16)], -1
    ).reshape(batch_count, row_count, 2 * HEAD_SIZE)
    window = [passed_along(pairs, "fsdp", o * stride) for o in range(back, 0, -1)] + [pairs]
    window = jnp.concatenate(window, 1)
    keys, values = window[..., :HEAD_SIZE], window[..., HEAD_SIZE:]

    cut = lambda array, b: array[b * row_count : (b + 1) * row_count]
    grads_in = [queue_gather(out_grad[b]) for b in batches]
    allowed, heads, totals, middle_own, middle = [], [], [], [], []
    for b in batches:
        allowed.append(allowed_keys(positions[b], row_count, back))
        heads_b, total_b = attend_forward(
            cut(query_rotated, b), keys[b], values[b], allowed[b], score_scale
        )
        heads.append(heads_b)
        totals.append(total_b)
        attn_own = tp_scatter_sum(dot_nn(heads_b.reshape(row_count, query_width), out_weight))
        middle_own.append(tokens[b].astype(F32) + attn_own)
        middle.append(tp_gather(middle_own[b].astype(BF16)).astype(F32))

    outputs, scale_two, normed_two, activated, grad_pair, grad_normed_two = [], [], [], [], [], []
    for b in batches:
        scale_two.append(
            lax.rsqrt(jnp.mean(middle[b] * middle[b], -1, keepdims=True) + NORM_EPSILON)
        )
        normed_two.append((middle[b] * scale_two[b] * gain_two).astype(BF16))
        both = dot_nn(normed_two[b], gate_up_weight)
        gate, up_proj = both[:, :hidden], both[:, hidden:]
        sigmoid_gate = jax.nn.sigmoid(gate)
        activated.append((gate * sigmoid_gate * up_proj).astype(BF16))
        grad_act = dot_nn(grads_in[b], down_weight.T)
        grad_gate_low = (
            grad_act * up_proj * sigmoid_gate * (1.0 + gate * (1.0 - sigmoid_gate))
        ).astype(BF16)
        grad_up_low = (grad_act * gate * sigmoid_gate).astype(BF16)
        grad_pair.append(jnp.concatenate([grad_gate_low, grad_up_low], 1))
        grad_normed_two.append(
            queue_gather(queue_scatter_sum(dot_nt(grad_pair[b], gate_up_weight)))
        )
    for b in batches:
        mlp_own = queue_scatter_sum(dot_nn(activated[b], down_weight))
        outputs.append((middle_own[b] + mlp_own.astype(F32)).astype(BF16))

    activated_all = jnp.concatenate(activated, 0)
    grads_in_all = jnp.concatenate(grads_in, 0)
    down_sum = owner_sums(lambda f: dot_tn(activated_all, owner_block(grads_in_all, f, 1)))
    normed_two_all = jnp.concatenate(normed_two, 0)
    grad_pair_all = jnp.concatenate(grad_pair, 0)
    pair_sum = owner_sums(lambda f: dot_tn(owner_block(normed_two_all, f, 1), grad_pair_all))

    gain_one_own = lax.dynamic_slice_in_dim(gain_one, column_start, local_width, 0)
    norm_sum_one = jnp.zeros((full_width,), F32)
    norm_sum_two = jnp.zeros((full_width,), F32)
    input_grads, middle_low, grad_projected = [], [], []
    for b in batches:
        grad_two = grad_normed_two[b].astype(F32)
        norm_sum_two = norm_sum_two + jnp.sum(grad_two * middle[b] * scale_two[b], 0)
        scaled_two = grad_two * gain_two
        grad_middle = (
            grads_in[b].astype(F32)
            + scale_two[b] * scaled_two
            - middle[b]
            * (scale_two[b] * scale_two[b] * scale_two[b])
            * jnp.mean(scaled_two * middle[b], -1, keepdims=True)
        )
        middle_low.append(grad_middle.astype(BF16))
        grad_heads = (
            dot_nt(middle_low[b], out_weight)
            .astype(BF16)
            .reshape(row_count, head_count, HEAD_SIZE)
        )
        grad_query_rot, grad_keys, grad_values = attend_backward(
            cut(query_rotated, b),
            keys[b],
            values[b],
            allowed[b],
            totals[b],
            heads[b],
            grad_heads,
            score_scale,
        )
        grad_window = jnp.concatenate([grad_keys, grad_values], -1)
        own_pairs = grad_window[back * row_count :]
        for o in range(1, back + 1):
            block = grad_window[(back - o) * row_count : (back - o + 1) * row_count]
            own_pairs = own_pairs + passed_along(
                block.astype(BF16), "fsdp", -o * stride
            ).astype(F32)
        cosine_b, sine_b = cut(cosine_table, b), cut(sine_lookup, b)
        grad_query_low = (
            reverse_rotary(grad_query_rot, cosine_b, sine_b)
            .reshape(row_count, query_width)
            .astype(BF16)
        )
        grad_key_low = reverse_rotary(own_pairs[:, None, :HEAD_SIZE], cosine_b, sine_b)[
            :, 0
        ].astype(BF16)
        grad_value_low = own_pairs[:, HEAD_SIZE:].astype(BF16)
        grad_projected.append(
            jnp.concatenate([grad_query_low, grad_key_low, grad_value_low], 1)
        )
        grad_one = dot_nt(grad_projected[b], project_weight)
        weighted = grad_one * inputs[b]
        norm_sum_one = norm_sum_one + jnp.sum(weighted * scale_one[b], 0)
        row_term = jnp.sum(weighted * gain_one, -1, keepdims=True) / full_width
        row_high = row_term.astype(BF16)
        row_low = (row_term - row_high.astype(F32)).astype(BF16)
        extra = jnp.pad(
            jnp.concatenate([row_high, row_low], 1), ((0, 0), (0, GAIN_COLUMNS - 2))
        )
        slots = grad_one.astype(BF16).reshape(row_count, -1, local_width)
        extra = jnp.broadcast_to(extra[:, None], (row_count, slots.shape[1], GAIN_COLUMNS))
        summed = queue_scatter_sum(jnp.concatenate([slots, extra], 2).reshape(row_count, -1))
        row_mean = jnp.sum(summed[:, local_width : local_width + 2].astype(F32), 1, keepdims=True)
        grad_middle_own = lax.dynamic_slice_in_dim(grad_middle, column_start, local_width, 1)
        input_grads.append(
            grad_middle_own
            + scale_one[b] * (summed[:, :local_width].astype(F32) * gain_one_own)
            - tokens[b].astype(F32) * (scale_one[b] * scale_one[b] * scale_one[b]) * row_mean
        )
    heads_all = jnp.concatenate([h.reshape(row_count, query_width) for h in heads], 0)
    middle_low_all = jnp.concatenate(middle_low, 0)
    out_sum = owner_sums(lambda f: dot_tn(heads_all, owner_block(middle_low_all, f, 1)))
    grad_projected_all = jnp.concatenate(grad_projected, 0)
    project_sum = owner_sums(
        lambda f: dot_tn(owner_block(normed_one, f, 1), grad_projected_all)
    )
    norm_sum_one = lax.psum(norm_sum_one, ("fsdp", "tp"))
    norm_sum_two = lax.psum(norm_sum_two, "fsdp")
    index = lax.axis_index("fsdp")
    grad_scale = (batch_count * row_count * lax.axis_size("fsdp")) ** (-0.5)
    return (
        jnp.stack(outputs),
        jnp.stack(input_grads),
        owner_block(norm_sum_one, index, 0) * grad_scale,
        project_sum[:, :query_width] * grad_scale,
        project_sum[:, query_width : query_width + HEAD_SIZE] * grad_scale,
        project_sum[:, query_width + HEAD_SIZE :] * grad_scale,
        out_sum * grad_scale,
        owner_block(norm_sum_two, index, 0) * grad_scale,
        pair_sum[:, :hidden] * grad_scale,
        pair_sum[:, hidden:] * grad_scale,
        down_sum * grad_scale,
    )


def solution(mesh):
    in_specs = (
        P(None, "fsdp", "tp"),
        P(None, "fsdp", "tp"),
        P(None, "fsdp"),
        P(None, "fsdp"),
        P("fsdp"),
        P("fsdp", "tp"),
        P("fsdp", "tp"),
        P("fsdp", "tp"),
        P("tp", "fsdp"),
        P("fsdp"),
        P("fsdp", "tp"),
        P("fsdp", "tp"),
        P("tp", "fsdp"),
    )
    out_specs = (
        P(None, "fsdp", "tp"),
        P(None, "fsdp", "tp"),
        P("fsdp"),
        P("fsdp", "tp"),
        P("fsdp", "tp"),
        P("fsdp", "tp"),
        P("tp", "fsdp"),
        P("fsdp"),
        P("fsdp", "tp"),
        P("fsdp", "tp"),
        P("tp", "fsdp"),
    )
    return jax.shard_map(shards, mesh=mesh, in_specs=in_specs, out_specs=out_specs, check_vma=False)
```

```python
import jax
import jax.numpy as jnp
from jax import lax
from jax.sharding import PartitionSpec as P

HEAD_SIZE = 64
SEQUENCE_LENGTH = 2048
DOC_MAX = 1024


NORM_EPSILON = 1e-05
ROPE_BASE = 10000.0
MASKED_SCORE = -1e30
GAIN_COLUMNS = 128

F32 = jnp.float32
BF16 = jnp.bfloat16


def rope_tables(offsets, head_width):
    half_width = head_width // 2
    inverse = ROPE_BASE ** (-(jnp.arange(half_width, dtype=F32) * 2.0 / head_width))
    angles = offsets.astype(F32)[:, None] * inverse[None, :]
    cosine_table = jnp.concatenate([jnp.cos(angles), jnp.cos(angles)], -1)
    sine_lookup = jnp.concatenate([jnp.sin(angles), jnp.sin(angles)], -1)
    return (cosine_table, sine_lookup)


def apply_rotary(vectors, cosine_table, sine_lookup):
    half_width = vectors.shape[-1] // 2
    turned = jnp.concatenate([-vectors[..., half_width:], vectors[..., :half_width]], -1)
    return vectors * cosine_table[:, None, :] + turned * sine_lookup[:, None, :]


def reverse_rotary(cotangent, cosine_table, sine_lookup):
    half_width = cotangent.shape[-1] // 2
    scaled = cotangent * sine_lookup[:, None, :]
    return cotangent * cosine_table[:, None, :] + jnp.concatenate(
        [scaled[..., half_width:], -scaled[..., :half_width]], -1
    )


def dot_nn(left, right):
    return jnp.dot(left, right, preferred_element_type=F32)


def dot_nt(left, right):
    return lax.dot_general(left, right, (((1,), (1,)), ((), ())), preferred_element_type=F32)


def dot_tn(left, right):
    return lax.dot_general(left, right, (((0,), (0,)), ((), ())), preferred_element_type=F32)


def exchange(block, axis, mask):
    return lax.ppermute(block, axis, [(i, i ^ mask) for i in range(lax.axis_size(axis))])


def passed_along(block, axis, distance):
    devices = range(lax.axis_size(axis))
    route = [(i - distance, i) for i in devices if i - distance in devices]
    return lax.ppermute(block, axis, route)


def tp_gather(part, *earlier):
    size = lax.axis_size("tp")
    index = lax.axis_index("tp")
    held = [part]
    bit = size // 2
    while bit:
        send = held[0][None] if len(held) == 1 else jnp.stack(held)
        other = exchange(send, "tp", bit)
        if earlier and bit > 1:
            other = after(other, *earlier)
        low = (index & bit) == 0
        merged = []
        for slot, block in enumerate(held):
            merged.append(jnp.where(low, block, other[slot]))
            merged.append(jnp.where(low, other[slot], block))
        held = merged
        bit //= 2
    return jnp.concatenate(held, 1)


def tp_scatter_sum(partial):
    size = lax.axis_size("tp")
    index = lax.axis_index("tp")
    width = partial.shape[1] // size
    held = [partial[:, s * width : (s + 1) * width] for s in range(size)]
    bit = 1
    while bit < size:
        low = (index & bit) == 0
        send = jnp.stack(
            [jnp.where(low, b, a).astype(BF16) for a, b in zip(held[0::2], held[1::2])]
        )
        other = exchange(send, "tp", bit)
        held = [
            jnp.where(low, a, b) + other[slot].astype(F32)
            for slot, (a, b) in enumerate(zip(held[0::2], held[1::2]))
        ]
        bit *= 2
    return held[0]


def queue_gather(part):
    return lax.all_gather(part, "tp", axis=1, tiled=True)


def queue_scatter_sum(partial):
    return lax.psum_scatter(partial.astype(BF16), "tp", scatter_dimension=1, tiled=True)


def owner_order(array):
    size = lax.axis_size("fsdp")
    index = lax.axis_index("fsdp")
    width = array.shape[1] // size
    cut = lambda owner: lax.dynamic_slice_in_dim(array, owner * width, width, 1)
    away = jnp.concatenate([cut(index ^ 1 ^ (2 * m)) for m in range(size // 2)], 1)
    return lax.optimization_barrier([away] + [cut(index ^ (2 * m)) for m in range(size // 2)])


def owner_terms(blocks, terms_of, axis):
    away = terms_of(blocks[0]).astype(BF16)
    other = exchange(away, "fsdp", 1)
    width = away.shape[axis] // (len(blocks) - 1)
    terms = []
    for m, block in enumerate(blocks[1:]):
        term = terms_of(block)
        term = term + lax.slice_in_dim(other, m * width, (m + 1) * width, axis=axis).astype(F32)
        terms.append(exchange(term.astype(BF16), "fsdp", 2 * m) if m else term)
    return terms


def owner_total(terms, *earlier):
    terms = lax.optimization_barrier(tuple(terms) + earlier)[: len(terms)]
    return sum(term.astype(F32) for term in terms)


def after(value, *earlier):
    return lax.optimization_barrier((value,) + earlier)[0]


def allowed_keys(offsets, row_count, back):
    row = jnp.arange(row_count, dtype=jnp.int32)[:, None] + back * row_count
    first = row - offsets[..., None]
    key = jnp.arange((back + 1) * row_count, dtype=jnp.int32)[None, :]
    return ((key >= first) & (key <= row))[:, None]


def attend_forward(query_rotated, keys, values, allowed, score_scale):
    scores = (
        jnp.einsum("blhd,bmd->bhlm", query_rotated, keys, preferred_element_type=F32)
        * score_scale
    )
    scores = jnp.where(allowed, scores, MASKED_SCORE)
    row_max = jnp.max(scores, -1)
    row_sum = jnp.sum(jnp.where(allowed, jnp.exp(scores - row_max[..., None]), 0.0), -1)
    log_total = row_max + jnp.log(row_sum)
    prob_round = jnp.where(allowed, jnp.exp(scores - log_total[..., None]), 0.0).astype(BF16)
    heads = jnp.einsum("bhlm,bmd->blhd", prob_round, values, preferred_element_type=F32)
    return (heads.astype(BF16), log_total)


def attend_backward(
    query_rotated, keys, values, allowed, log_total, heads_low, grad_low, score_scale
):
    delta = jnp.swapaxes(jnp.sum(grad_low.astype(F32) * heads_low.astype(F32), -1), 1, 2)
    scores = (
        jnp.einsum("blhd,bmd->bhlm", query_rotated, keys, preferred_element_type=F32)
        * score_scale
    )
    prob_exact = jnp.where(allowed, jnp.exp(scores - log_total[..., None]), 0.0)
    prob_round = prob_exact.astype(BF16)
    grad_values = jnp.einsum("bhlm,blhd->bmd", prob_round, grad_low, preferred_element_type=F32)
    grad_probs = jnp.einsum("blhd,bmd->bhlm", grad_low, values, preferred_element_type=F32)
    grad_scores = (prob_exact * (grad_probs - delta[..., None]) * score_scale).astype(BF16)
    grad_query = jnp.einsum("bhlm,bmd->blhd", grad_scores, keys, preferred_element_type=F32)
    grad_keys = jnp.einsum(
        "bhlm,blhd->bmd", grad_scores, query_rotated, preferred_element_type=F32
    )
    return (grad_query, grad_keys, grad_values)


def shards(
    tokens,
    out_grad,
    segment_ids,
    positions,
    attn_norm,
    w_query,
    key_projection_weight,
    value_projection_weight,
    w_out,
    mlp_norm,
    w_gate,
    w_up,
    w_down,
):
    batch_count, row_count, local_width = tokens.shape
    full_width = local_width * lax.axis_size("tp")
    group_size = SEQUENCE_LENGTH // row_count
    stride = lax.axis_size("fsdp") // group_size
    query_width = w_query.shape[1]
    hidden = w_gate.shape[1]
    head_count = query_width // HEAD_SIZE
    score_scale = HEAD_SIZE ** (-0.5)
    back = min(group_size - 1, -(-(DOC_MAX - 1) // row_count))
    column_start = lax.axis_index("tp") * local_width
    shard_rows = w_query.shape[0]

    gains = jnp.stack([attn_norm, mlp_norm], 1)
    gains = jnp.pad(gains, ((0, 0), (0, GAIN_COLUMNS - 2)))
    first_shard = jnp.concatenate(
        [w_query, key_projection_weight, value_projection_weight, gains], 1
    )
    project_width = query_width + 2 * HEAD_SIZE
    first_full = lax.all_gather(first_shard, "fsdp", axis=0, tiled=True)
    project_weight = first_full[:, :project_width]
    gain_rows = first_full[:, project_width : project_width + 2].astype(F32).T
    gain_one, gain_two = gain_rows[0], gain_rows[1]
    rows = batch_count * row_count
    tokens_own = tokens.reshape(rows, local_width)
    tokens_full = tp_gather(tokens_own)
    out_weight = lax.all_gather(after(w_out, tokens_full), "fsdp", axis=1, tiled=True)
    gate_up_shard = lax.optimization_barrier(jnp.concatenate([w_gate, w_up], 1))
    gate_up_weight = lax.all_gather(
        after(gate_up_shard, tokens_full), "fsdp", axis=0, tiled=True
    )
    down_weight = lax.all_gather(after(w_down, tokens_full), "fsdp", axis=1, tiled=True)

    by_batch = lambda array: array.reshape((batch_count, row_count) + array.shape[1:])
    all_rows = lambda array: array.reshape((rows,) + array.shape[2:])
    inputs = tokens_full.astype(F32)
    scale_one = lax.rsqrt(jnp.mean(inputs * inputs, -1, keepdims=True) + NORM_EPSILON)
    normed_one = (inputs * scale_one * gain_one).astype(BF16)
    projected = dot_nn(normed_one, project_weight)
    tables = rope_tables(positions.reshape(rows), HEAD_SIZE)
    allowed = allowed_keys(positions, row_count, back)
    query_rotated = by_batch(
        apply_rotary(
            projected[:, :query_width].reshape(rows, head_count, HEAD_SIZE), *tables
        ).astype(BF16)
    )
    key_rotated = apply_rotary(
        projected[:, None, query_width : query_width + HEAD_SIZE], *tables
    )[:, 0].astype(BF16)
    pairs = by_batch(
        jnp.concatenate([key_rotated, projected[:, query_width + HEAD_SIZE :].astype(BF16)], -1)
    )
    grad_in = tp_gather(after(out_grad.reshape(rows, local_width), tokens_full), pairs)
    window = [passed_along(pairs, "fsdp", o * stride) for o in range(back, 0, -1)]
    window = jnp.concatenate(window + [pairs], 1)
    keys, values = window[..., :HEAD_SIZE], window[..., HEAD_SIZE:]
    heads, totals = attend_forward(query_rotated, keys, values, allowed, score_scale)
    heads_out = heads.reshape(rows, query_width)
    middle_own = tokens_own.astype(F32) + tp_scatter_sum(
        dot_nn(after(heads_out, grad_in), out_weight)
    )
    middle = tp_gather(middle_own.astype(BF16)).astype(F32)

    scale_two = lax.rsqrt(jnp.mean(middle * middle, -1, keepdims=True) + NORM_EPSILON)
    normed_two = lax.optimization_barrier((middle * scale_two * gain_two).astype(BF16))
    both = dot_nn(normed_two, gate_up_weight)
    gate, up_proj = both[:, :hidden], both[:, hidden:]
    sigmoid_gate = jax.nn.sigmoid(gate)
    activated = (gate * sigmoid_gate * up_proj).astype(BF16)
    grad_act = dot_nn(grad_in, down_weight.T)
    grad_gate_low = (
        grad_act * up_proj * sigmoid_gate * (1.0 + gate * (1.0 - sigmoid_gate))
    ).astype(BF16)
    grad_up_low = (grad_act * gate * sigmoid_gate).astype(BF16)
    grad_normed_two = queue_gather(
        queue_scatter_sum(
            dot_nt(grad_gate_low, gate_up_weight[:, :hidden])
            + dot_nt(grad_up_low, gate_up_weight[:, hidden:])
        )
    )
    mlp_own = queue_scatter_sum(after(dot_nn(activated, down_weight).astype(BF16), grad_normed_two))
    output = (middle_own + mlp_own.astype(F32)).astype(BF16)

    normed_two_order = owner_order(normed_two)
    gate_terms = owner_terms(normed_two_order, lambda block: dot_tn(block, grad_gate_low), 0)
    up_terms = owner_terms(normed_two_order, lambda block: dot_tn(block, grad_up_low), 0)

    gain_one_own = lax.dynamic_slice_in_dim(gain_one, column_start, local_width, 0)
    grad_two = grad_normed_two.astype(F32)
    norm_sum_two = jnp.sum(grad_two * middle * scale_two, 0)
    scaled_two = grad_two * gain_two
    grad_middle = (
        grad_in.astype(F32)
        + scale_two * scaled_two
        - middle
        * (scale_two * scale_two * scale_two)
        * jnp.mean(scaled_two * middle, -1, keepdims=True)
    )
    middle_low = lax.optimization_barrier(grad_middle.astype(BF16))
    grad_heads = by_batch(
        dot_nt(middle_low, out_weight).astype(BF16).reshape(rows, head_count, HEAD_SIZE)
    )
    grad_query_rot, grad_keys, grad_values = attend_backward(
        query_rotated, keys, values, allowed, totals, heads, grad_heads, score_scale
    )
    grad_window = jnp.concatenate([grad_keys, grad_values], -1)
    own_pairs = grad_window[:, back * row_count :]
    for o in range(1, back + 1):
        block = grad_window[:, (back - o) * row_count : (back - o + 1) * row_count]
        own_pairs = own_pairs + passed_along(block.astype(BF16), "fsdp", -o * stride).astype(F32)
    own_pairs = all_rows(own_pairs)
    grads_order = owner_order(after(grad_in, own_pairs))
    down_terms = owner_terms(grads_order, lambda block: dot_tn(activated, block), 1)
    grad_query_low = (
        reverse_rotary(all_rows(grad_query_rot), *tables).reshape(rows, query_width).astype(BF16)
    )
    grad_key_low = reverse_rotary(own_pairs[:, None, :HEAD_SIZE], *tables)[:, 0].astype(BF16)
    grad_value_low = own_pairs[:, HEAD_SIZE:].astype(BF16)
    grad_projected = after(
        jnp.concatenate([grad_query_low, grad_key_low, grad_value_low], 1), mlp_own
    )
    grad_one = dot_nt(grad_projected, project_weight)
    weighted = grad_one * inputs
    norm_sum_one = jnp.sum(weighted * scale_one, 0)
    summed = queue_scatter_sum(grad_one)
    small = jnp.concatenate([norm_sum_one, jnp.sum(weighted * gain_one, -1) / full_width])
    for bit in range((lax.axis_size("tp") - 1).bit_length()):
        small = small + exchange(small, "tp", 1 << bit)
    norm_sum_one, row_mean = small[:full_width], small[full_width:, None]
    grad_middle_own = lax.dynamic_slice_in_dim(grad_middle, column_start, local_width, 1)
    input_grad = (
        grad_middle_own
        + scale_one * (summed.astype(F32) * gain_one_own)
        - tokens_own.astype(F32) * (scale_one * scale_one * scale_one) * row_mean
    )
    middle_order = owner_order(middle_low)
    out_terms = owner_terms(middle_order, lambda block: dot_tn(heads_out, block), 1)
    norm_order = owner_order(jnp.stack([norm_sum_one, norm_sum_two]))
    normed_one_order = owner_order(normed_one)
    project_terms = owner_terms(
        list(zip(normed_one_order, norm_order)),
        lambda pair: jnp.concatenate(
            [
                dot_tn(pair[0], grad_projected),
                jnp.pad(pair[1].T, ((0, 0), (0, GAIN_COLUMNS - 2))),
            ],
            1,
        ),
        0,
    )
    grad_scale = (batch_count * row_count * lax.axis_size("fsdp")) ** (-0.5)
    down_sum = owner_total(down_terms, grad_projected)
    gate_sum = owner_total(gate_terms, grad_projected)
    up_sum = owner_total(up_terms, grad_projected)
    out_sum = owner_total(out_terms, grad_projected)
    project_sum = owner_total(project_terms) * grad_scale
    return (
        by_batch(output),
        by_batch(input_grad),
        project_sum[:, project_width],
        project_sum[:, :query_width],
        project_sum[:, query_width : query_width + HEAD_SIZE],
        project_sum[:, query_width + HEAD_SIZE : project_width],
        out_sum * grad_scale,
        project_sum[:, project_width + 1],
        gate_sum * grad_scale,
        up_sum * grad_scale,
        down_sum * grad_scale,
    )


def solution(mesh):
    in_specs = (
        P(None, "fsdp", "tp"),
        P(None, "fsdp", "tp"),
        P(None, "fsdp"),
        P(None, "fsdp"),
        P("fsdp"),
        P("fsdp", "tp"),
        P("fsdp", "tp"),
        P("fsdp", "tp"),
        P("tp", "fsdp"),
        P("fsdp"),
        P("fsdp", "tp"),
        P("fsdp", "tp"),
        P("tp", "fsdp"),
    )
    out_specs = (
        P(None, "fsdp", "tp"),
        P(None, "fsdp", "tp"),
        P("fsdp"),
        P("fsdp", "tp"),
        P("fsdp", "tp"),
        P("fsdp", "tp"),
        P("tp", "fsdp"),
        P("fsdp"),
        P("fsdp", "tp"),
        P("fsdp", "tp"),
        P("tp", "fsdp"),
    )
    return jax.shard_map(shards, mesh=mesh, in_specs=in_specs, out_specs=out_specs, check_vma=False)
```

```python
import jax
import jax.numpy as jnp
from jax import lax
from jax.sharding import PartitionSpec as P


HEAD_SIZE = 64
SEQUENCE_LENGTH = 2048
DOC_MAX = 1024


NORM_EPSILON = 1e-05
ROPE_BASE = 10000.0
MASKED_SCORE = -1e30
GAIN_COLUMNS = 128

F32 = jnp.float32
BF16 = jnp.bfloat16


def rope_tables(offsets, head_width):
    half_width = head_width // 2
    inverse = ROPE_BASE ** (-(jnp.arange(half_width, dtype=F32) * 2.0 / head_width))
    angles = offsets.astype(F32)[:, None] * inverse[None, :]
    cosine_table = jnp.concatenate([jnp.cos(angles), jnp.cos(angles)], -1)
    sine_lookup = jnp.concatenate([jnp.sin(angles), jnp.sin(angles)], -1)
    return (cosine_table, sine_lookup)


def apply_rotary(vectors, cosine_table, sine_lookup):
    half_width = vectors.shape[-1] // 2
    turned = jnp.concatenate([-vectors[..., half_width:], vectors[..., :half_width]], -1)
    return vectors * cosine_table[:, None, :] + turned * sine_lookup[:, None, :]


def reverse_rotary(cotangent, cosine_table, sine_lookup):
    half_width = cotangent.shape[-1] // 2
    scaled = cotangent * sine_lookup[:, None, :]
    return cotangent * cosine_table[:, None, :] + jnp.concatenate(
        [scaled[..., half_width:], -scaled[..., :half_width]], -1
    )


def dot_nn(left, right):
    return jnp.dot(left, right, preferred_element_type=F32)


def dot_nt(left, right):
    return lax.dot_general(left, right, (((1,), (1,)), ((), ())), preferred_element_type=F32)


def dot_tn(left, right):
    return lax.dot_general(left, right, (((0,), (0,)), ((), ())), preferred_element_type=F32)


def exchange(block, axis, mask):
    return lax.ppermute(block, axis, [(i, i ^ mask) for i in range(lax.axis_size(axis))])


def passed_along(block, axis, distance):
    devices = range(lax.axis_size(axis))
    route = [(i - distance, i) for i in devices if i - distance in devices]
    return lax.ppermute(block, axis, route)


def tp_gather(part, *earlier):
    size = lax.axis_size("tp")
    index = lax.axis_index("tp")
    up, down = [part], [part]
    for step in range(1, size):
        lower, upper = up[-1], down[-1]
        if earlier and step == 2:
            lower, upper = after(lower, *earlier), after(upper, *earlier)
        up.append(lax.ppermute(lower, "tp", [(i, i + 1) for i in range(step - 1, size - 1)]))
        down.append(lax.ppermute(upper, "tp", [(i, i - 1) for i in range(1, size - step + 1)]))
    slots = []
    for slot in range(size):
        block = part
        for other in range(size):
            if other != slot:
                held = up[other - slot] if other > slot else down[slot - other]
                block = jnp.where(index == other, held, block)
        slots.append(block)
    return jnp.concatenate(slots, 1)


def tp_scatter_sum(partial):
    size = lax.axis_size("tp")
    index = lax.axis_index("tp")
    width = partial.shape[1] // size

    def slot(at):
        at = jnp.clip(at, 0, size - 1)
        return lax.dynamic_slice_in_dim(partial, at * width, width, 1)

    total = slot(index)
    lower = upper = None
    for step in range(1, size):
        to_upper, to_lower = slot(index + size - step), slot(index - size + step)
        if lower is not None:
            to_upper, to_lower = to_upper + lower.astype(F32), to_lower + upper.astype(F32)
        lower = lax.ppermute(
            to_upper.astype(BF16), "tp", [(i, i + 1) for i in range(min(step, size - 1))]
        )
        upper = lax.ppermute(
            to_lower.astype(BF16), "tp", [(i, i - 1) for i in range(size - step, size)]
        )
    return total + lower.astype(F32) + upper.astype(F32)


def queue_gather(part):
    return lax.all_gather(part, "tp", axis=1, tiled=True)


def queue_scatter_sum(partial):
    return lax.psum_scatter(partial.astype(BF16), "tp", scatter_dimension=1, tiled=True)


def owner_order(array):
    size = lax.axis_size("fsdp")
    index = lax.axis_index("fsdp")
    width = array.shape[1] // size
    cut = lambda owner: lax.dynamic_slice_in_dim(array, owner * width, width, 1)
    away = jnp.concatenate([cut(index ^ 1 ^ (2 * m)) for m in range(size // 2)], 1)
    return lax.optimization_barrier([away] + [cut(index ^ (2 * m)) for m in range(size // 2)])


def owner_terms(blocks, terms_of, axis):
    away = terms_of(blocks[0]).astype(BF16)
    other = exchange(away, "fsdp", 1)
    width = away.shape[axis] // (len(blocks) - 1)
    terms, sent = [], []
    for m, block in enumerate(blocks[1:]):
        share = lax.slice_in_dim(other, m * width, (m + 1) * width, axis=axis)
        term = terms_of(block) + share.astype(F32)
        if m:
            sent.append(term.astype(BF16))
        if m:
            term = exchange(sent[-1], "fsdp", 2 * m)
        terms.append(term)
    return terms, sent


def owner_total(terms, *earlier):
    terms = lax.optimization_barrier(tuple(terms) + earlier)[: len(terms)]
    return sum(term.astype(F32) for term in terms)


def after(value, *earlier):
    return lax.optimization_barrier((value,) + earlier)[0]


def allowed_keys(offsets, row_count, back):
    row = jnp.arange(row_count, dtype=jnp.int32)[:, None] + back * row_count
    first = row - offsets[..., None]
    key = jnp.arange((back + 1) * row_count, dtype=jnp.int32)[None, :]
    return ((key >= first) & (key <= row))[:, None]


def attend_forward(query_rotated, keys, values, allowed, score_scale):
    scores = (
        jnp.einsum("blhd,bmd->bhlm", query_rotated, keys, preferred_element_type=F32)
        * score_scale
    )
    scores = jnp.where(allowed, scores, MASKED_SCORE)
    row_max = jnp.max(scores, -1)
    row_sum = jnp.sum(jnp.where(allowed, jnp.exp(scores - row_max[..., None]), 0.0), -1)
    log_total = row_max + jnp.log(row_sum)
    prob_round = jnp.where(allowed, jnp.exp(scores - log_total[..., None]), 0.0).astype(BF16)
    heads = jnp.einsum("bhlm,bmd->blhd", prob_round, values, preferred_element_type=F32)
    return (heads.astype(BF16), log_total)


def attend_backward(
    query_rotated, keys, values, allowed, log_total, heads_low, grad_low, score_scale
):
    delta = jnp.swapaxes(jnp.sum(grad_low.astype(F32) * heads_low.astype(F32), -1), 1, 2)
    scores = (
        jnp.einsum("blhd,bmd->bhlm", query_rotated, keys, preferred_element_type=F32)
        * score_scale
    )
    prob_exact = jnp.where(allowed, jnp.exp(scores - log_total[..., None]), 0.0)
    prob_round = prob_exact.astype(BF16)
    grad_values = jnp.einsum("bhlm,blhd->bmd", prob_round, grad_low, preferred_element_type=F32)
    grad_probs = jnp.einsum("blhd,bmd->bhlm", grad_low, values, preferred_element_type=F32)
    grad_scores = (prob_exact * (grad_probs - delta[..., None]) * score_scale).astype(BF16)
    grad_query = jnp.einsum("bhlm,bmd->blhd", grad_scores, keys, preferred_element_type=F32)
    grad_keys = jnp.einsum(
        "bhlm,blhd->bmd", grad_scores, query_rotated, preferred_element_type=F32
    )
    return (grad_query, grad_keys, grad_values)


def shards(
    tokens,
    out_grad,
    segment_ids,
    positions,
    attn_norm,
    w_query,
    key_projection_weight,
    value_projection_weight,
    w_out,
    mlp_norm,
    w_gate,
    w_up,
    w_down,
):
    batch_count, row_count, local_width = tokens.shape
    full_width = local_width * lax.axis_size("tp")
    group_size = SEQUENCE_LENGTH // row_count
    stride = lax.axis_size("fsdp") // group_size
    query_width = w_query.shape[1]
    hidden = w_gate.shape[1]
    head_count = query_width // HEAD_SIZE
    score_scale = HEAD_SIZE ** (-0.5)
    back = min(group_size - 1, -(-(DOC_MAX - 1) // row_count))
    column_start = lax.axis_index("tp") * local_width

    gains = jnp.stack([attn_norm, mlp_norm], 1)
    gains = jnp.pad(gains, ((0, 0), (0, GAIN_COLUMNS - 2)))
    first_shard = jnp.concatenate(
        [w_query, key_projection_weight, value_projection_weight, gains], 1
    )
    project_width = query_width + 2 * HEAD_SIZE
    first_full = lax.all_gather(first_shard, "fsdp", axis=0, tiled=True)
    project_weight = first_full[:, :project_width]
    gain_rows = first_full[:, project_width : project_width + 2].astype(F32).T
    gain_one, gain_two = gain_rows[0], gain_rows[1]
    rows = batch_count * row_count
    tokens_own = tokens.reshape(rows, local_width)
    tokens_full = tp_gather(tokens_own)
    out_weight = lax.all_gather(after(w_out, tokens_full), "fsdp", axis=1, tiled=True)
    gate_up_shard = lax.optimization_barrier(jnp.concatenate([w_gate, w_up], 1))
    gate_up_weight = lax.all_gather(
        after(gate_up_shard, tokens_full), "fsdp", axis=0, tiled=True
    )
    down_weight = lax.all_gather(after(w_down, tokens_full), "fsdp", axis=1, tiled=True)

    by_batch = lambda array: array.reshape((batch_count, row_count) + array.shape[1:])
    all_rows = lambda array: array.reshape((rows,) + array.shape[2:])
    inputs = tokens_full.astype(F32)
    scale_one = lax.rsqrt(jnp.mean(inputs * inputs, -1, keepdims=True) + NORM_EPSILON)
    normed_one = (inputs * scale_one * gain_one).astype(BF16)
    projected = dot_nn(normed_one, project_weight)
    tables = rope_tables(positions.reshape(rows), HEAD_SIZE)
    allowed = allowed_keys(positions, row_count, back)
    query_rotated = by_batch(
        apply_rotary(
            projected[:, :query_width].reshape(rows, head_count, HEAD_SIZE), *tables
        ).astype(BF16)
    )
    key_rotated = apply_rotary(
        projected[:, None, query_width : query_width + HEAD_SIZE], *tables
    )[:, 0].astype(BF16)
    pairs = by_batch(
        jnp.concatenate([key_rotated, projected[:, query_width + HEAD_SIZE :].astype(BF16)], -1)
    )
    grad_in = tp_gather(after(out_grad.reshape(rows, local_width), tokens_full), pairs)
    window = [passed_along(pairs, "fsdp", o * stride) for o in range(back, 0, -1)]
    window = jnp.concatenate(window + [pairs], 1)
    keys, values = window[..., :HEAD_SIZE], window[..., HEAD_SIZE:]
    heads, totals = attend_forward(query_rotated, keys, values, allowed, score_scale)
    heads_out = heads.reshape(rows, query_width)
    middle_own = tokens_own.astype(F32) + tp_scatter_sum(
        dot_nn(after(heads_out, grad_in), out_weight)
    )
    middle = tp_gather(middle_own.astype(BF16)).astype(F32)

    scale_two = lax.rsqrt(jnp.mean(middle * middle, -1, keepdims=True) + NORM_EPSILON)
    normed_two = lax.optimization_barrier((middle * scale_two * gain_two).astype(BF16))
    both = dot_nn(normed_two, gate_up_weight)
    gate, up_proj = both[:, :hidden], both[:, hidden:]
    sigmoid_gate = jax.nn.sigmoid(gate)
    activated = (gate * sigmoid_gate * up_proj).astype(BF16)
    grad_act = dot_nn(grad_in, down_weight.T)
    grad_gate_low = (
        grad_act * up_proj * sigmoid_gate * (1.0 + gate * (1.0 - sigmoid_gate))
    ).astype(BF16)
    grad_up_low = (grad_act * gate * sigmoid_gate).astype(BF16)
    partial_two = queue_scatter_sum(
        dot_nt(grad_gate_low, gate_up_weight[:, :hidden])
        + dot_nt(grad_up_low, gate_up_weight[:, hidden:])
    )
    normed_two_order = owner_order(normed_two)
    gate_terms, gate_sent = owner_terms(
        normed_two_order, lambda block: dot_tn(block, grad_gate_low), 0
    )
    up_terms, up_sent = owner_terms(normed_two_order, lambda block: dot_tn(block, grad_up_low), 0)
    grads_order = owner_order(grad_in)
    down_terms, _ = owner_terms(grads_order, lambda block: dot_tn(activated, block), 1)
    grad_normed_two = queue_gather(after(partial_two, *gate_sent, *up_sent))
    mlp_own = queue_scatter_sum(after(dot_nn(activated, down_weight).astype(BF16), grad_normed_two))
    output = (middle_own + mlp_own.astype(F32)).astype(BF16)

    gain_one_own = lax.dynamic_slice_in_dim(gain_one, column_start, local_width, 0)
    grad_two = grad_normed_two.astype(F32)
    norm_sum_two = jnp.sum(grad_two * middle * scale_two, 0)
    scaled_two = grad_two * gain_two
    grad_middle = (
        grad_in.astype(F32)
        + scale_two * scaled_two
        - middle
        * (scale_two * scale_two * scale_two)
        * jnp.mean(scaled_two * middle, -1, keepdims=True)
    )
    middle_low = lax.optimization_barrier(grad_middle.astype(BF16))
    grad_heads = by_batch(
        dot_nt(middle_low, out_weight).astype(BF16).reshape(rows, head_count, HEAD_SIZE)
    )
    grad_query_rot, grad_keys, grad_values = attend_backward(
        query_rotated, keys, values, allowed, totals, heads, grad_heads, score_scale
    )
    grad_window = jnp.concatenate([grad_keys, grad_values], -1)
    own_pairs = grad_window[:, back * row_count :]
    for o in range(1, back + 1):
        block = grad_window[:, (back - o) * row_count : (back - o + 1) * row_count]
        own_pairs = own_pairs + passed_along(block.astype(BF16), "fsdp", -o * stride).astype(F32)
    own_pairs = all_rows(own_pairs)
    grad_query_low = (
        reverse_rotary(all_rows(grad_query_rot), *tables).reshape(rows, query_width).astype(BF16)
    )
    grad_key_low = reverse_rotary(own_pairs[:, None, :HEAD_SIZE], *tables)[:, 0].astype(BF16)
    grad_value_low = own_pairs[:, HEAD_SIZE:].astype(BF16)
    grad_projected = lax.optimization_barrier(
        jnp.concatenate([grad_query_low, grad_key_low, grad_value_low], 1)
    )
    grad_one = dot_nt(grad_projected, project_weight)
    weighted = grad_one * inputs
    norm_sum_one = jnp.sum(weighted * scale_one, 0)
    summed = queue_scatter_sum(after(grad_one.astype(BF16), mlp_own))
    small = jnp.concatenate([norm_sum_one, jnp.sum(weighted * gain_one, -1) / full_width])
    for bit in range((lax.axis_size("tp") - 1).bit_length()):
        small = small + exchange(small, "tp", 1 << bit)
    norm_sum_one, row_mean = small[:full_width], small[full_width:, None]
    grad_middle_own = lax.dynamic_slice_in_dim(grad_middle, column_start, local_width, 1)
    input_grad = (
        grad_middle_own
        + scale_one * (summed.astype(F32) * gain_one_own)
        - tokens_own.astype(F32) * (scale_one * scale_one * scale_one) * row_mean
    )
    middle_order = owner_order(middle_low)
    out_terms, _ = owner_terms(middle_order, lambda block: dot_tn(heads_out, block), 1)
    norm_order = owner_order(jnp.stack([norm_sum_one, norm_sum_two]))
    normed_one_order = owner_order(normed_one)
    project_terms, project_sent = owner_terms(
        list(zip(normed_one_order, norm_order)),
        lambda pair: jnp.concatenate(
            [
                dot_tn(pair[0], grad_projected),
                jnp.pad(pair[1].T, ((0, 0), (0, GAIN_COLUMNS - 2))),
            ],
            1,
        ),
        0,
    )
    grad_scale = (batch_count * row_count * lax.axis_size("fsdp")) ** (-0.5)
    down_sum = owner_total(down_terms, *project_sent)
    gate_sum = owner_total(gate_terms, *project_sent)
    up_sum = owner_total(up_terms, *project_sent)
    out_sum = owner_total(out_terms, *project_sent)
    project_sum = owner_total(project_terms) * grad_scale
    return (
        by_batch(output),
        by_batch(input_grad),
        project_sum[:, project_width],
        project_sum[:, :query_width],
        project_sum[:, query_width : query_width + HEAD_SIZE],
        project_sum[:, query_width + HEAD_SIZE : project_width],
        out_sum * grad_scale,
        project_sum[:, project_width + 1],
        gate_sum * grad_scale,
        up_sum * grad_scale,
        down_sum * grad_scale,
    )


def solution(mesh):
    in_specs = (
        P(None, "fsdp", "tp"),
        P(None, "fsdp", "tp"),
        P(None, "fsdp"),
        P(None, "fsdp"),
        P("fsdp"),
        P("fsdp", "tp"),
        P("fsdp", "tp"),
        P("fsdp", "tp"),
        P("tp", "fsdp"),
        P("fsdp"),
        P("fsdp", "tp"),
        P("fsdp", "tp"),
        P("tp", "fsdp"),
    )
    out_specs = (
        P(None, "fsdp", "tp"),
        P(None, "fsdp", "tp"),
        P("fsdp"),
        P("fsdp", "tp"),
        P("fsdp", "tp"),
        P("fsdp", "tp"),
        P("tp", "fsdp"),
        P("fsdp"),
        P("fsdp", "tp"),
        P("fsdp", "tp"),
        P("tp", "fsdp"),
    )

    return jax.shard_map(shards, mesh=mesh, in_specs=in_specs, out_specs=out_specs, check_vma=False)
```

```python
import jax
import jax.numpy as jnp
from jax import lax
from jax.sharding import PartitionSpec as P


HEAD_SIZE = 64
SEQUENCE_LENGTH = 2048
DOC_MAX = 1024


NORM_EPSILON = 1e-05
ROPE_BASE = 10000.0
MASKED_SCORE = -1e30
GAIN_COLUMNS = 128

F32 = jnp.float32
BF16 = jnp.bfloat16


def rope_tables(offsets, head_width):
    half_width = head_width // 2
    inverse = ROPE_BASE ** (-(jnp.arange(half_width, dtype=F32) * 2.0 / head_width))
    angles = offsets.astype(F32)[:, None] * inverse[None, :]
    cosine_table = jnp.concatenate([jnp.cos(angles), jnp.cos(angles)], -1)
    sine_lookup = jnp.concatenate([jnp.sin(angles), jnp.sin(angles)], -1)
    return (cosine_table, sine_lookup)


def apply_rotary(vectors, cosine_table, sine_lookup):
    half_width = vectors.shape[-1] // 2
    turned = jnp.concatenate([-vectors[..., half_width:], vectors[..., :half_width]], -1)
    return vectors * cosine_table[:, None, :] + turned * sine_lookup[:, None, :]


def reverse_rotary(cotangent, cosine_table, sine_lookup):
    half_width = cotangent.shape[-1] // 2
    scaled = cotangent * sine_lookup[:, None, :]
    return cotangent * cosine_table[:, None, :] + jnp.concatenate(
        [scaled[..., half_width:], -scaled[..., :half_width]], -1
    )


def dot_nn(left, right):
    return jnp.dot(left, right, preferred_element_type=F32)


def dot_nt(left, right):
    return lax.dot_general(left, right, (((1,), (1,)), ((), ())), preferred_element_type=F32)


def dot_tn(left, right):
    return lax.dot_general(left, right, (((0,), (0,)), ((), ())), preferred_element_type=F32)


def exchange(block, axis, mask):
    return lax.ppermute(block, axis, [(i, i ^ mask) for i in range(lax.axis_size(axis))])


def passed_along(block, axis, distance):
    devices = range(lax.axis_size(axis))
    route = [(i - distance, i) for i in devices if i - distance in devices]
    return lax.ppermute(block, axis, route)


def tp_gather(part, *earlier):
    size = lax.axis_size("tp")
    index = lax.axis_index("tp")
    up, down = [part], [part]
    for step in range(1, size):
        lower, upper = up[-1], down[-1]
        if 2 <= step < len(earlier) + 2:
            lower, upper = lax.optimization_barrier((lower, upper, earlier[step - 2]))[:2]
        up.append(lax.ppermute(lower, "tp", [(i, i + 1) for i in range(step - 1, size - 1)]))
        down.append(lax.ppermute(upper, "tp", [(i, i - 1) for i in range(1, size - step + 1)]))
    slots = []
    for slot in range(size):
        block = part
        for other in range(size):
            if other != slot:
                held = up[other - slot] if other > slot else down[slot - other]
                block = jnp.where(index == other, held, block)
        slots.append(block)
    return jnp.concatenate(slots, 1)


def tp_gather_far(part, *earlier):
    size = lax.axis_size("tp")
    index = lax.axis_index("tp")
    held = [part]
    bit = size // 2
    while bit:
        send = held[0][None] if len(held) == 1 else jnp.stack(held)
        other = exchange(send, "tp", bit)
        if earlier and bit > 1:
            other = after(other, *earlier)
        low = (index & bit) == 0
        merged = []
        for slot, block in enumerate(held):
            merged.append(jnp.where(low, block, other[slot]))
            merged.append(jnp.where(low, other[slot], block))
        held = merged
        bit //= 2
    return jnp.concatenate(held, 1)


def tp_scatter_sum(partial):
    size = lax.axis_size("tp")
    index = lax.axis_index("tp")
    width = partial.shape[1] // size
    held = [partial[:, s * width : (s + 1) * width] for s in range(size)]
    bit = 1
    while bit < size:
        low = (index & bit) == 0
        send = jnp.stack(
            [jnp.where(low, b, a).astype(BF16) for a, b in zip(held[0::2], held[1::2])]
        )
        other = exchange(send, "tp", bit)
        held = [
            jnp.where(low, a, b) + other[slot].astype(F32)
            for slot, (a, b) in enumerate(zip(held[0::2], held[1::2]))
        ]
        bit *= 2
    return held[0]


def queue_gather(part):
    return lax.all_gather(part, "tp", axis=1, tiled=True)


def queue_scatter_sum(partial):
    return lax.psum_scatter(partial.astype(BF16), "tp", scatter_dimension=1, tiled=True)


def owner_order(array):
    size = lax.axis_size("fsdp")
    index = lax.axis_index("fsdp")
    width = array.shape[1] // size
    cut = lambda owner: lax.dynamic_slice_in_dim(array, owner * width, width, 1)
    away = jnp.concatenate([cut(index ^ 1 ^ (2 * m)) for m in range(size // 2)], 1)
    return lax.optimization_barrier([away] + [cut(index ^ (2 * m)) for m in range(size // 2)])


def owner_terms(blocks, terms_of, axis):
    away = terms_of(blocks[0]).astype(BF16)
    other = exchange(away, "fsdp", 1)
    width = away.shape[axis] // (len(blocks) - 1)
    terms, sent = [], []
    for m, block in enumerate(blocks[1:]):
        share = lax.slice_in_dim(other, m * width, (m + 1) * width, axis=axis)
        term = terms_of(block) + share.astype(F32)
        if m:
            sent.append(term.astype(BF16))
        if m:
            term = exchange(sent[-1], "fsdp", 2 * m)
        terms.append(term)
    return terms, sent


def owner_total(terms, *earlier):
    terms = lax.optimization_barrier(tuple(terms) + earlier)[: len(terms)]
    return sum(term.astype(F32) for term in terms)


def after(value, *earlier):
    return lax.optimization_barrier((value,) + earlier)[0]


def allowed_keys(offsets, row_count, back):
    row = jnp.arange(row_count, dtype=jnp.int32)[:, None] + back * row_count
    first = row - offsets[..., None]
    key = jnp.arange((back + 1) * row_count, dtype=jnp.int32)[None, :]
    return ((key >= first) & (key <= row))[:, None]


def attend_forward(query_rotated, keys, values, allowed, score_scale):
    scores = (
        jnp.einsum("blhd,bmd->bhlm", query_rotated, keys, preferred_element_type=F32)
        * score_scale
    )
    scores = jnp.where(allowed, scores, MASKED_SCORE)
    row_max = jnp.max(scores, -1)
    row_sum = jnp.sum(jnp.where(allowed, jnp.exp(scores - row_max[..., None]), 0.0), -1)
    log_total = row_max + jnp.log(row_sum)
    prob_round = jnp.where(allowed, jnp.exp(scores - log_total[..., None]), 0.0).astype(BF16)
    heads = jnp.einsum("bhlm,bmd->blhd", prob_round, values, preferred_element_type=F32)
    return (heads.astype(BF16), log_total)


def attend_backward(
    query_rotated, keys, values, allowed, log_total, heads_low, grad_low, score_scale
):
    delta = jnp.swapaxes(jnp.sum(grad_low.astype(F32) * heads_low.astype(F32), -1), 1, 2)
    scores = (
        jnp.einsum("blhd,bmd->bhlm", query_rotated, keys, preferred_element_type=F32)
        * score_scale
    )
    prob_exact = jnp.where(allowed, jnp.exp(scores - log_total[..., None]), 0.0)
    prob_round = prob_exact.astype(BF16)
    grad_values = jnp.einsum("bhlm,blhd->bmd", prob_round, grad_low, preferred_element_type=F32)
    grad_probs = jnp.einsum("blhd,bmd->bhlm", grad_low, values, preferred_element_type=F32)
    grad_scores = (prob_exact * (grad_probs - delta[..., None]) * score_scale).astype(BF16)
    grad_query = jnp.einsum("bhlm,bmd->blhd", grad_scores, keys, preferred_element_type=F32)
    grad_keys = jnp.einsum(
        "bhlm,blhd->bmd", grad_scores, query_rotated, preferred_element_type=F32
    )
    return (grad_query, grad_keys, grad_values)


def shards(
    tokens,
    out_grad,
    segment_ids,
    positions,
    attn_norm,
    w_query,
    key_projection_weight,
    value_projection_weight,
    w_out,
    mlp_norm,
    w_gate,
    w_up,
    w_down,
):
    batch_count, row_count, local_width = tokens.shape
    full_width = local_width * lax.axis_size("tp")
    group_size = SEQUENCE_LENGTH // row_count
    stride = lax.axis_size("fsdp") // group_size
    query_width = w_query.shape[1]
    hidden = w_gate.shape[1]
    head_count = query_width // HEAD_SIZE
    score_scale = HEAD_SIZE ** (-0.5)
    back = min(group_size - 1, -(-(DOC_MAX - 1) // row_count))
    column_start = lax.axis_index("tp") * local_width
    shard_rows = w_query.shape[0]

    gains = jnp.stack([attn_norm, mlp_norm], 1)
    gains = jnp.pad(gains, ((0, 0), (0, GAIN_COLUMNS - 2)))
    first_shard = jnp.concatenate(
        [w_query, key_projection_weight, value_projection_weight, gains], 1
    )
    project_width = query_width + 2 * HEAD_SIZE
    first_full = lax.all_gather(first_shard, "fsdp", axis=0, tiled=True)
    project_weight = first_full[:, :project_width]
    gain_rows = first_full[:, project_width : project_width + 2].astype(F32).T
    gain_one, gain_two = gain_rows[0], gain_rows[1]
    rows = batch_count * row_count
    tokens_own = tokens.reshape(rows, local_width)
    gate_up_shard = lax.optimization_barrier(jnp.concatenate([w_gate, w_up], 1))
    tables, allowed, gain_one, gain_two = lax.optimization_barrier(
        (
            rope_tables(positions.reshape(rows), HEAD_SIZE),
            allowed_keys(positions, row_count, back),
            gain_one,
            gain_two,
        )
    )
    tokens_full = tp_gather(tokens_own, gate_up_shard, gain_one)
    out_weight = lax.all_gather(after(w_out, tokens_full), "fsdp", axis=1, tiled=True)
    gate_up_weight = lax.all_gather(
        after(gate_up_shard, tokens_full), "fsdp", axis=0, tiled=True
    )
    down_weight = lax.all_gather(after(w_down, tokens_full), "fsdp", axis=1, tiled=True)

    by_batch = lambda array: array.reshape((batch_count, row_count) + array.shape[1:])
    all_rows = lambda array: array.reshape((rows,) + array.shape[2:])
    inputs = tokens_full.astype(F32)
    scale_one = lax.rsqrt(jnp.mean(inputs * inputs, -1, keepdims=True) + NORM_EPSILON)
    normed_one = (inputs * scale_one * gain_one).astype(BF16)
    projected = dot_nn(normed_one, project_weight)
    query_rotated = by_batch(
        apply_rotary(
            projected[:, :query_width].reshape(rows, head_count, HEAD_SIZE), *tables
        ).astype(BF16)
    )
    key_rotated = apply_rotary(
        projected[:, None, query_width : query_width + HEAD_SIZE], *tables
    )[:, 0].astype(BF16)
    pairs = by_batch(
        jnp.concatenate([key_rotated, projected[:, query_width + HEAD_SIZE :].astype(BF16)], -1)
    )
    grad_in = tp_gather_far(after(out_grad.reshape(rows, local_width), tokens_full), pairs)
    window = [passed_along(pairs, "fsdp", o * stride) for o in range(back, 0, -1)]
    window = jnp.concatenate(window + [pairs], 1)
    keys, values = window[..., :HEAD_SIZE], window[..., HEAD_SIZE:]
    heads, totals = attend_forward(query_rotated, keys, values, allowed, score_scale)
    heads_out = heads.reshape(rows, query_width)
    middle_own = tokens_own.astype(F32) + tp_scatter_sum(
        dot_nn(after(heads_out, grad_in), out_weight)
    )
    middle = tp_gather(middle_own.astype(BF16)).astype(F32)

    scale_two = lax.rsqrt(jnp.mean(middle * middle, -1, keepdims=True) + NORM_EPSILON)
    normed_two = lax.optimization_barrier((middle * scale_two * gain_two).astype(BF16))
    both = dot_nn(normed_two, gate_up_weight)
    gate, up_proj = both[:, :hidden], both[:, hidden:]
    sigmoid_gate = jax.nn.sigmoid(gate)
    activated = (gate * sigmoid_gate * up_proj).astype(BF16)
    grad_act = dot_nn(grad_in, down_weight.T)
    grad_gate_low = (
        grad_act * up_proj * sigmoid_gate * (1.0 + gate * (1.0 - sigmoid_gate))
    ).astype(BF16)
    grad_up_low = (grad_act * gate * sigmoid_gate).astype(BF16)
    partial_two = queue_scatter_sum(
        dot_nt(grad_gate_low, gate_up_weight[:, :hidden])
        + dot_nt(grad_up_low, gate_up_weight[:, hidden:])
    )
    normed_two_order = owner_order(normed_two)
    gate_terms, gate_sent = owner_terms(
        normed_two_order, lambda block: dot_tn(block, grad_gate_low), 0
    )
    up_terms, up_sent = owner_terms(normed_two_order, lambda block: dot_tn(block, grad_up_low), 0)
    grads_order = owner_order(grad_in)
    down_terms, _ = owner_terms(grads_order, lambda block: dot_tn(activated, block), 1)
    grad_normed_two = queue_gather(after(partial_two, *gate_sent, *up_sent))
    mlp_partial = dot_nn(activated, down_weight).astype(BF16)
    mlp_own = queue_scatter_sum(after(mlp_partial, grad_normed_two))
    output = (middle_own + mlp_own.astype(F32)).astype(BF16)

    gain_one_own = lax.dynamic_slice_in_dim(gain_one, column_start, local_width, 0)
    grad_two = grad_normed_two.astype(F32)
    norm_sum_two = jnp.sum(grad_two * middle * scale_two, 0)
    scaled_two = grad_two * gain_two
    grad_middle = (
        grad_in.astype(F32)
        + scale_two * scaled_two
        - middle
        * (scale_two * scale_two * scale_two)
        * jnp.mean(scaled_two * middle, -1, keepdims=True)
    )
    middle_low = lax.optimization_barrier(grad_middle.astype(BF16))
    grad_heads = by_batch(
        dot_nt(middle_low, out_weight).astype(BF16).reshape(rows, head_count, HEAD_SIZE)
    )
    grad_query_rot, grad_keys, grad_values = attend_backward(
        query_rotated, keys, values, allowed, totals, heads, grad_heads, score_scale
    )
    grad_window = jnp.concatenate([grad_keys, grad_values], -1)
    own_pairs = grad_window[:, back * row_count :]
    for o in range(1, back + 1):
        block = grad_window[:, (back - o) * row_count : (back - o + 1) * row_count]
        own_pairs = own_pairs + passed_along(block.astype(BF16), "fsdp", -o * stride).astype(F32)
    own_pairs = all_rows(own_pairs)
    grad_query_low = (
        reverse_rotary(all_rows(grad_query_rot), *tables).reshape(rows, query_width).astype(BF16)
    )
    grad_key_low = reverse_rotary(own_pairs[:, None, :HEAD_SIZE], *tables)[:, 0].astype(BF16)
    grad_value_low = own_pairs[:, HEAD_SIZE:].astype(BF16)
    grad_projected = lax.optimization_barrier(
        jnp.concatenate([grad_query_low, grad_key_low, grad_value_low], 1)
    )
    grad_one = dot_nt(grad_projected, project_weight)
    weighted = grad_one * inputs
    norm_sum_one = jnp.sum(weighted * scale_one, 0)
    summed = queue_scatter_sum(after(grad_one.astype(BF16), mlp_own))
    small = jnp.concatenate([norm_sum_one, jnp.sum(weighted * gain_one, -1) / full_width])
    for bit in range((lax.axis_size("tp") - 1).bit_length()):
        small = small + exchange(small, "tp", 1 << bit)
    row_mean = small[full_width:, None]
    norm_sums = jnp.concatenate([small[:full_width], norm_sum_two])
    for bit in range((lax.axis_size("fsdp") - 1).bit_length()):
        norm_sums = norm_sums + exchange(norm_sums, "fsdp", 1 << bit)
    grad_middle_own = lax.dynamic_slice_in_dim(grad_middle, column_start, local_width, 1)
    input_grad = (
        grad_middle_own
        + scale_one * (summed.astype(F32) * gain_one_own)
        - tokens_own.astype(F32) * (scale_one * scale_one * scale_one) * row_mean
    )
    normed_one_order = owner_order(normed_one)
    project_terms, project_sent = owner_terms(
        normed_one_order, lambda block: dot_tn(block, grad_projected), 0
    )
    middle_order = owner_order(after(middle_low, *project_sent))
    out_terms, out_sent = owner_terms(middle_order, lambda block: dot_tn(heads_out, block), 1)
    grad_scale = (batch_count * row_count * lax.axis_size("fsdp")) ** (-0.5)
    norm_start = lax.axis_index("fsdp") * shard_rows
    norm_sums = norm_sums * grad_scale
    down_sum = owner_total(down_terms, *out_sent)
    gate_sum = owner_total(gate_terms, *out_sent)
    up_sum = owner_total(up_terms, *out_sent)
    out_sum = owner_total(out_terms, *out_sent)
    project_sum = owner_total(project_terms) * grad_scale
    return (
        by_batch(output),
        by_batch(input_grad),
        lax.dynamic_slice_in_dim(norm_sums, norm_start, shard_rows, 0),
        project_sum[:, :query_width],
        project_sum[:, query_width : query_width + HEAD_SIZE],
        project_sum[:, query_width + HEAD_SIZE :],
        out_sum * grad_scale,
        lax.dynamic_slice_in_dim(norm_sums, full_width + norm_start, shard_rows, 0),
        gate_sum * grad_scale,
        up_sum * grad_scale,
        down_sum * grad_scale,
    )


def solution(mesh):
    in_specs = (
        P(None, "fsdp", "tp"),
        P(None, "fsdp", "tp"),
        P(None, "fsdp"),
        P(None, "fsdp"),
        P("fsdp"),
        P("fsdp", "tp"),
        P("fsdp", "tp"),
        P("fsdp", "tp"),
        P("tp", "fsdp"),
        P("fsdp"),
        P("fsdp", "tp"),
        P("fsdp", "tp"),
        P("tp", "fsdp"),
    )
    out_specs = (
        P(None, "fsdp", "tp"),
        P(None, "fsdp", "tp"),
        P("fsdp"),
        P("fsdp", "tp"),
        P("fsdp", "tp"),
        P("fsdp", "tp"),
        P("tp", "fsdp"),
        P("fsdp"),
        P("fsdp", "tp"),
        P("fsdp", "tp"),
        P("tp", "fsdp"),
    )

    return jax.shard_map(shards, mesh=mesh, in_specs=in_specs, out_specs=out_specs, check_vma=False)
```

```python
import jax
import jax.numpy as jnp
from jax import lax
from jax.sharding import PartitionSpec as P


HEAD_SIZE = 64
SEQUENCE_LENGTH = 2048
DOC_MAX = 1024


NORM_EPSILON = 1e-05
ROPE_BASE = 10000.0
MASKED_SCORE = -1e30
GAIN_COLUMNS = 128

F32 = jnp.float32
BF16 = jnp.bfloat16


def rope_tables(offsets, head_width):
    half_width = head_width // 2
    inverse = ROPE_BASE ** (-(jnp.arange(half_width, dtype=F32) * 2.0 / head_width))
    angles = offsets.astype(F32)[:, None] * inverse[None, :]
    cosine_table = jnp.concatenate([jnp.cos(angles), jnp.cos(angles)], -1)
    sine_lookup = jnp.concatenate([jnp.sin(angles), jnp.sin(angles)], -1)
    return (cosine_table, sine_lookup)


def apply_rotary(vectors, cosine_table, sine_lookup):
    half_width = vectors.shape[-1] // 2
    turned = jnp.concatenate([-vectors[..., half_width:], vectors[..., :half_width]], -1)
    return vectors * cosine_table[:, None, :] + turned * sine_lookup[:, None, :]


def reverse_rotary(cotangent, cosine_table, sine_lookup):
    half_width = cotangent.shape[-1] // 2
    scaled = cotangent * sine_lookup[:, None, :]
    return cotangent * cosine_table[:, None, :] + jnp.concatenate(
        [scaled[..., half_width:], -scaled[..., :half_width]], -1
    )


def dot_nn(left, right):
    return jnp.dot(left, right, preferred_element_type=F32)


def dot_nt(left, right):
    return lax.dot_general(left, right, (((1,), (1,)), ((), ())), preferred_element_type=F32)


def dot_tn(left, right):
    return lax.dot_general(left, right, (((0,), (0,)), ((), ())), preferred_element_type=F32)


def exchange(block, axis, mask):
    return lax.ppermute(block, axis, [(i, i ^ mask) for i in range(lax.axis_size(axis))])


def passed_along(block, axis, distance):
    devices = range(lax.axis_size(axis))
    route = [(i - distance, i) for i in devices if i - distance in devices]
    return lax.ppermute(block, axis, route)


def tp_gather(part, *earlier):
    size = lax.axis_size("tp")
    index = lax.axis_index("tp")
    up, down = [part], [part]
    for step in range(1, size):
        lower, upper = up[-1], down[-1]
        if 2 <= step < len(earlier) + 2:
            lower, upper = lax.optimization_barrier((lower, upper, earlier[step - 2]))[:2]
        up.append(lax.ppermute(lower, "tp", [(i, i + 1) for i in range(step - 1, size - 1)]))
        down.append(lax.ppermute(upper, "tp", [(i, i - 1) for i in range(1, size - step + 1)]))
    slots = []
    for slot in range(size):
        block = part
        for other in range(size):
            if other != slot:
                held = up[other - slot] if other > slot else down[slot - other]
                block = jnp.where(index == other, held, block)
        slots.append(block)
    return jnp.concatenate(slots, 1)


def tp_gather_far(part, *earlier):
    size = lax.axis_size("tp")
    index = lax.axis_index("tp")
    held = [part]
    bit = size // 2
    while bit:
        send = held[0][None] if len(held) == 1 else jnp.stack(held)
        other = exchange(send, "tp", bit)
        if earlier and bit > 1:
            other = after(other, *earlier)
        low = (index & bit) == 0
        merged = []
        for slot, block in enumerate(held):
            merged.append(jnp.where(low, block, other[slot]))
            merged.append(jnp.where(low, other[slot], block))
        held = merged
        bit //= 2
    return jnp.concatenate(held, 1)


def tp_scatter_sum(partial, *late):
    size = lax.axis_size("tp")
    index = lax.axis_index("tp")
    width = partial.shape[1] // size
    held = [partial[:, s * width : (s + 1) * width] for s in range(size)]
    bit = 1
    while bit < size:
        low = (index & bit) == 0
        send = jnp.stack(
            [jnp.where(low, b, a).astype(BF16) for a, b in zip(held[0::2], held[1::2])]
        )
        other = exchange(send, "tp", bit)
        if late and 2 * bit >= size:
            other = after(other, *late)
        held = [
            jnp.where(low, a, b) + other[slot].astype(F32)
            for slot, (a, b) in enumerate(zip(held[0::2], held[1::2]))
        ]
        bit *= 2
    return held[0]


def queue_gather(part):
    return lax.all_gather(part, "tp", axis=1, tiled=True)


def queue_scatter_sum(partial):
    return lax.psum_scatter(partial.astype(BF16), "tp", scatter_dimension=1, tiled=True)


def owner_order(array):
    size = lax.axis_size("fsdp")
    index = lax.axis_index("fsdp")
    width = array.shape[1] // size
    cut = lambda owner: lax.dynamic_slice_in_dim(array, owner * width, width, 1)
    away = jnp.concatenate([cut(index ^ 1 ^ (2 * m)) for m in range(size // 2)], 1)
    return lax.optimization_barrier([away] + [cut(index ^ (2 * m)) for m in range(size // 2)])


def owner_terms(blocks, terms_of, axis):
    away = terms_of(blocks[0]).astype(BF16)
    other = exchange(away, "fsdp", 1)
    width = away.shape[axis] // (len(blocks) - 1)
    terms, sent = [], []
    for m, block in enumerate(blocks[1:]):
        share = lax.slice_in_dim(other, m * width, (m + 1) * width, axis=axis)
        term = terms_of(block) + share.astype(F32)
        if m:
            sent.append(term.astype(BF16))
        if m:
            term = exchange(sent[-1], "fsdp", 2 * m)
        terms.append(term)
    return terms, sent


def owner_total(terms, *earlier):
    terms = lax.optimization_barrier(tuple(terms) + earlier)[: len(terms)]
    return sum(term.astype(F32) for term in terms)


def after(value, *earlier):
    return lax.optimization_barrier((value,) + earlier)[0]


def allowed_keys(offsets, row_count, back):
    row = jnp.arange(row_count, dtype=jnp.int32)[:, None] + back * row_count
    first = row - offsets[..., None]
    key = jnp.arange((back + 1) * row_count, dtype=jnp.int32)[None, :]
    return ((key >= first) & (key <= row))[:, None]


def attend_forward(query_rotated, keys, values, allowed, score_scale):
    scores = (
        jnp.einsum("blhd,bmd->bhlm", query_rotated, keys, preferred_element_type=F32)
        * score_scale
    )
    scores = jnp.where(allowed, scores, MASKED_SCORE)
    row_max = jnp.max(scores, -1)
    row_sum = jnp.sum(jnp.where(allowed, jnp.exp(scores - row_max[..., None]), 0.0), -1)
    log_total = row_max + jnp.log(row_sum)
    prob_round = jnp.where(allowed, jnp.exp(scores - log_total[..., None]), 0.0).astype(BF16)
    heads = jnp.einsum("bhlm,bmd->blhd", prob_round, values, preferred_element_type=F32)
    return (heads.astype(BF16), log_total)


def attention_weights(query_rotated, keys, allowed, log_total, score_scale):
    scores = (
        jnp.einsum("blhd,bmd->bhlm", query_rotated, keys, preferred_element_type=F32)
        * score_scale
    )
    weights = jnp.where(allowed, jnp.exp(scores - log_total[..., None]), 0.0).astype(BF16)
    return lax.optimization_barrier(weights)


def attend_backward(query_rotated, keys, values, weights, heads_low, grad_low, score_scale):
    delta = jnp.swapaxes(jnp.sum(grad_low.astype(F32) * heads_low.astype(F32), -1), 1, 2)
    grad_values = jnp.einsum("bhlm,blhd->bmd", weights, grad_low, preferred_element_type=F32)
    grad_probs = jnp.einsum("blhd,bmd->bhlm", grad_low, values, preferred_element_type=F32)
    grad_scores = (
        weights.astype(F32) * (grad_probs - delta[..., None]) * score_scale
    ).astype(BF16)
    grad_query = jnp.einsum("bhlm,bmd->blhd", grad_scores, keys, preferred_element_type=F32)
    grad_keys = jnp.einsum(
        "bhlm,blhd->bmd", grad_scores, query_rotated, preferred_element_type=F32
    )
    return (grad_query, grad_keys, grad_values)


def shards(
    tokens,
    out_grad,
    segment_ids,
    positions,
    attn_norm,
    w_query,
    key_projection_weight,
    value_projection_weight,
    w_out,
    mlp_norm,
    w_gate,
    w_up,
    w_down,
):
    batch_count, row_count, local_width = tokens.shape
    full_width = local_width * lax.axis_size("tp")
    group_size = SEQUENCE_LENGTH // row_count
    stride = lax.axis_size("fsdp") // group_size
    query_width = w_query.shape[1]
    hidden = w_gate.shape[1]
    head_count = query_width // HEAD_SIZE
    score_scale = HEAD_SIZE ** (-0.5)
    back = min(group_size - 1, -(-(DOC_MAX - 1) // row_count))
    column_start = lax.axis_index("tp") * local_width
    shard_rows = w_query.shape[0]

    gains = jnp.stack([attn_norm, mlp_norm], 1)
    gains = jnp.pad(gains, ((0, 0), (0, GAIN_COLUMNS - 2)))
    first_shard = jnp.concatenate(
        [w_query, key_projection_weight, value_projection_weight, gains], 1
    )
    project_width = query_width + 2 * HEAD_SIZE
    first_full = lax.all_gather(first_shard, "fsdp", axis=0, tiled=True)
    project_weight = first_full[:, :project_width]
    gain_rows = first_full[:, project_width : project_width + 2].astype(F32).T
    gain_one, gain_two = gain_rows[0], gain_rows[1]
    rows = batch_count * row_count
    tokens_own = tokens.reshape(rows, local_width)
    gate_up_shard = lax.optimization_barrier(jnp.concatenate([w_gate, w_up], 1))
    tables, allowed, gain_one, gain_two = lax.optimization_barrier(
        (
            rope_tables(positions.reshape(rows), HEAD_SIZE),
            allowed_keys(positions, row_count, back),
            gain_one,
            gain_two,
        )
    )
    tokens_full = tp_gather(tokens_own, gate_up_shard, gain_one)
    out_weight = lax.all_gather(after(w_out, tokens_full), "fsdp", axis=1, tiled=True)
    gate_up_weight = lax.all_gather(
        after(gate_up_shard, tokens_full), "fsdp", axis=0, tiled=True
    )
    down_weight = lax.all_gather(after(w_down, tokens_full), "fsdp", axis=1, tiled=True)

    by_batch = lambda array: array.reshape((batch_count, row_count) + array.shape[1:])
    all_rows = lambda array: array.reshape((rows,) + array.shape[2:])
    inputs = tokens_full.astype(F32)
    scale_one = lax.rsqrt(jnp.mean(inputs * inputs, -1, keepdims=True) + NORM_EPSILON)
    normed_one = (inputs * scale_one * gain_one).astype(BF16)
    projected = dot_nn(normed_one, project_weight)
    query_rotated = by_batch(
        apply_rotary(
            projected[:, :query_width].reshape(rows, head_count, HEAD_SIZE), *tables
        ).astype(BF16)
    )
    key_rotated = apply_rotary(
        projected[:, None, query_width : query_width + HEAD_SIZE], *tables
    )[:, 0].astype(BF16)
    pairs = by_batch(
        jnp.concatenate([key_rotated, projected[:, query_width + HEAD_SIZE :].astype(BF16)], -1)
    )
    grad_in = tp_gather_far(after(out_grad.reshape(rows, local_width), tokens_full), pairs)
    window = [passed_along(pairs, "fsdp", o * stride) for o in range(back, 0, -1)]
    window = jnp.concatenate(window + [pairs], 1)
    keys, values = window[..., :HEAD_SIZE], window[..., HEAD_SIZE:]
    heads, totals = attend_forward(query_rotated, keys, values, allowed, score_scale)
    heads_out = heads.reshape(rows, query_width)
    middle_own = tokens_own.astype(F32) + tp_scatter_sum(
        dot_nn(after(heads_out, grad_in), out_weight)
    )
    middle = tp_gather(middle_own.astype(BF16)).astype(F32)

    scale_two = lax.rsqrt(jnp.mean(middle * middle, -1, keepdims=True) + NORM_EPSILON)
    normed_two = lax.optimization_barrier((middle * scale_two * gain_two).astype(BF16))
    both = dot_nn(normed_two, gate_up_weight)
    gate, up_proj = both[:, :hidden], both[:, hidden:]
    sigmoid_gate = jax.nn.sigmoid(gate)
    activated = (gate * sigmoid_gate * up_proj).astype(BF16)
    grad_act = dot_nn(grad_in, down_weight.T)
    grad_gate_low = (
        grad_act * up_proj * sigmoid_gate * (1.0 + gate * (1.0 - sigmoid_gate))
    ).astype(BF16)
    grad_up_low = (grad_act * gate * sigmoid_gate).astype(BF16)
    partial_two = queue_scatter_sum(
        dot_nt(grad_gate_low, gate_up_weight[:, :hidden])
        + dot_nt(grad_up_low, gate_up_weight[:, hidden:])
    )
    normed_two_order = owner_order(normed_two)
    gate_terms, gate_sent = owner_terms(
        normed_two_order, lambda block: dot_tn(block, grad_gate_low), 0
    )
    up_terms, up_sent = owner_terms(normed_two_order, lambda block: dot_tn(block, grad_up_low), 0)
    grads_order = owner_order(grad_in)
    down_terms, _ = owner_terms(grads_order, lambda block: dot_tn(activated, block), 1)
    grad_normed_two = queue_gather(after(partial_two, *gate_sent, *up_sent))
    weights = attention_weights(
        after(query_rotated, grad_up_low), keys, allowed, totals, score_scale
    )
    mlp_partial = dot_nn(activated, down_weight).astype(BF16)
    mlp_own = queue_scatter_sum(after(mlp_partial, grad_normed_two))
    output = (middle_own + mlp_own.astype(F32)).astype(BF16)

    gain_one_own = lax.dynamic_slice_in_dim(gain_one, column_start, local_width, 0)
    grad_two = grad_normed_two.astype(F32)
    norm_sum_two = jnp.sum(grad_two * middle * scale_two, 0)
    scaled_two = grad_two * gain_two
    grad_middle = (
        grad_in.astype(F32)
        + scale_two * scaled_two
        - middle
        * (scale_two * scale_two * scale_two)
        * jnp.mean(scaled_two * middle, -1, keepdims=True)
    )
    middle_low = lax.optimization_barrier(grad_middle.astype(BF16))
    grad_heads = by_batch(
        dot_nt(middle_low, out_weight).astype(BF16).reshape(rows, head_count, HEAD_SIZE)
    )
    grad_query_rot, grad_keys, grad_values = attend_backward(
        query_rotated, keys, values, weights, heads, grad_heads, score_scale
    )
    grad_window = jnp.concatenate([grad_keys, grad_values], -1)
    own_pairs = grad_window[:, back * row_count :]
    for o in range(1, back + 1):
        block = grad_window[:, (back - o) * row_count : (back - o + 1) * row_count]
        own_pairs = own_pairs + passed_along(block.astype(BF16), "fsdp", -o * stride).astype(F32)
    own_pairs = all_rows(own_pairs)
    grad_query_low = (
        reverse_rotary(all_rows(grad_query_rot), *tables).reshape(rows, query_width).astype(BF16)
    )
    grad_key_low = reverse_rotary(own_pairs[:, None, :HEAD_SIZE], *tables)[:, 0].astype(BF16)
    grad_value_low = own_pairs[:, HEAD_SIZE:].astype(BF16)
    grad_projected = lax.optimization_barrier(
        jnp.concatenate([grad_query_low, grad_key_low, grad_value_low], 1)
    )
    normed_one_order = owner_order(normed_one)
    project_terms, project_sent = owner_terms(
        normed_one_order, lambda block: dot_tn(block, grad_projected), 0
    )
    grad_one = dot_nt(grad_projected, project_weight)
    weighted = grad_one * inputs
    norm_sum_one = jnp.sum(weighted * scale_one, 0)
    summed = by_batch(after(grad_one.astype(BF16), mlp_own))
    summed = [queue_scatter_sum(summed[0]), summed[1:].reshape(rows - row_count, full_width)]
    summed[1] = tp_scatter_sum(summed[1].astype(F32), *project_sent)
    summed = jnp.concatenate([block.astype(F32) for block in summed])
    small = jnp.concatenate([norm_sum_one, jnp.sum(weighted * gain_one, -1) / full_width])
    for bit in range((lax.axis_size("tp") - 1).bit_length()):
        small = small + exchange(small, "tp", 1 << bit)
    row_mean = small[full_width:, None]
    norm_sums = jnp.concatenate([small[:full_width], norm_sum_two])
    for bit in range((lax.axis_size("fsdp") - 1).bit_length()):
        norm_sums = norm_sums + exchange(norm_sums, "fsdp", 1 << bit)
    grad_middle_own = lax.dynamic_slice_in_dim(grad_middle, column_start, local_width, 1)
    input_grad = (
        grad_middle_own
        + scale_one * (summed * gain_one_own)
        - tokens_own.astype(F32) * (scale_one * scale_one * scale_one) * row_mean
    )
    middle_order = owner_order(after(middle_low, *project_sent))
    out_terms, _ = owner_terms(middle_order, lambda block: dot_tn(heads_out, block), 1)
    grad_scale = (batch_count * row_count * lax.axis_size("fsdp")) ** (-0.5)
    norm_start = lax.axis_index("fsdp") * shard_rows
    norm_sums = norm_sums * grad_scale
    down_sum = owner_total(down_terms, *project_sent)
    gate_sum = owner_total(gate_terms, *project_sent)
    up_sum = owner_total(up_terms, *project_sent)
    out_sum = owner_total(out_terms)
    project_sum = owner_total(project_terms) * grad_scale
    return (
        by_batch(output),
        by_batch(input_grad),
        lax.dynamic_slice_in_dim(norm_sums, norm_start, shard_rows, 0),
        project_sum[:, :query_width],
        project_sum[:, query_width : query_width + HEAD_SIZE],
        project_sum[:, query_width + HEAD_SIZE :],
        out_sum * grad_scale,
        lax.dynamic_slice_in_dim(norm_sums, full_width + norm_start, shard_rows, 0),
        gate_sum * grad_scale,
        up_sum * grad_scale,
        down_sum * grad_scale,
    )


def solution(mesh):
    in_specs = (
        P(None, "fsdp", "tp"),
        P(None, "fsdp", "tp"),
        P(None, "fsdp"),
        P(None, "fsdp"),
        P("fsdp"),
        P("fsdp", "tp"),
        P("fsdp", "tp"),
        P("fsdp", "tp"),
        P("tp", "fsdp"),
        P("fsdp"),
        P("fsdp", "tp"),
        P("fsdp", "tp"),
        P("tp", "fsdp"),
    )
    out_specs = (
        P(None, "fsdp", "tp"),
        P(None, "fsdp", "tp"),
        P("fsdp"),
        P("fsdp", "tp"),
        P("fsdp", "tp"),
        P("fsdp", "tp"),
        P("tp", "fsdp"),
        P("fsdp"),
        P("fsdp", "tp"),
        P("fsdp", "tp"),
        P("tp", "fsdp"),
    )

    return jax.shard_map(shards, mesh=mesh, in_specs=in_specs, out_specs=out_specs, check_vma=False)
```

```python
import jax
import jax.numpy as jnp
from jax import lax
from jax.sharding import PartitionSpec as P


HEAD_SIZE = 64
SEQUENCE_LENGTH = 2048
DOC_MAX = 1024


NORM_EPSILON = 1e-05
ROPE_BASE = 10000.0
MASKED_SCORE = -1e30
GAIN_COLUMNS = 128

F32 = jnp.float32
BF16 = jnp.bfloat16


def rope_tables(offsets, head_width):
    half_width = head_width // 2
    inverse = ROPE_BASE ** (-(jnp.arange(half_width, dtype=F32) * 2.0 / head_width))
    angles = offsets.astype(F32)[:, None] * inverse[None, :]
    cosine_table = jnp.concatenate([jnp.cos(angles), jnp.cos(angles)], -1)
    sine_lookup = jnp.concatenate([jnp.sin(angles), jnp.sin(angles)], -1)
    return (cosine_table, sine_lookup)


def apply_rotary(vectors, cosine_table, sine_lookup):
    half_width = vectors.shape[-1] // 2
    turned = jnp.concatenate([-vectors[..., half_width:], vectors[..., :half_width]], -1)
    return vectors * cosine_table[:, None, :] + turned * sine_lookup[:, None, :]


def reverse_rotary(cotangent, cosine_table, sine_lookup):
    half_width = cotangent.shape[-1] // 2
    scaled = cotangent * sine_lookup[:, None, :]
    return cotangent * cosine_table[:, None, :] + jnp.concatenate(
        [scaled[..., half_width:], -scaled[..., :half_width]], -1
    )


def dot_nn(left, right):
    return jnp.dot(left, right, preferred_element_type=F32)


def dot_nt(left, right):
    return lax.dot_general(left, right, (((1,), (1,)), ((), ())), preferred_element_type=F32)


def dot_tn(left, right):
    return lax.dot_general(left, right, (((0,), (0,)), ((), ())), preferred_element_type=F32)


def exchange(block, axis, mask):
    return lax.ppermute(block, axis, [(i, i ^ mask) for i in range(lax.axis_size(axis))])


def passed_along(block, axis, distance):
    devices = range(lax.axis_size(axis))
    route = [(i - distance, i) for i in devices if i - distance in devices]
    return lax.ppermute(block, axis, route)


def tp_gather(part, *earlier):
    size = lax.axis_size("tp")
    index = lax.axis_index("tp")
    up, down = [part], [part]
    for step in range(1, size):
        lower, upper = up[-1], down[-1]
        if 2 <= step < len(earlier) + 2:
            lower, upper = lax.optimization_barrier((lower, upper, earlier[step - 2]))[:2]
        up.append(lax.ppermute(lower, "tp", [(i, i + 1) for i in range(step - 1, size - 1)]))
        down.append(lax.ppermute(upper, "tp", [(i, i - 1) for i in range(1, size - step + 1)]))
    slots = []
    for slot in range(size):
        block = part
        for other in range(size):
            if other != slot:
                held = up[other - slot] if other > slot else down[slot - other]
                block = jnp.where(index == other, held, block)
        slots.append(block)
    return jnp.concatenate(slots, 1)


def tp_gather_far(part, *earlier):
    size = lax.axis_size("tp")
    index = lax.axis_index("tp")
    held = [part]
    bit = size // 2
    while bit:
        send = held[0][None] if len(held) == 1 else jnp.stack(held)
        other = exchange(send, "tp", bit)
        if earlier and bit > 1:
            other = after(other, *earlier)
        low = (index & bit) == 0
        merged = []
        for slot, block in enumerate(held):
            merged.append(jnp.where(low, block, other[slot]))
            merged.append(jnp.where(low, other[slot], block))
        held = merged
        bit //= 2
    return jnp.concatenate(held, 1)


def tp_scatter_sum(partial, *late):
    size = lax.axis_size("tp")
    index = lax.axis_index("tp")
    width = partial.shape[1] // size
    held = [partial[:, s * width : (s + 1) * width] for s in range(size)]
    bit = 1
    while bit < size:
        low = (index & bit) == 0
        send = jnp.stack(
            [jnp.where(low, b, a).astype(BF16) for a, b in zip(held[0::2], held[1::2])]
        )
        other = exchange(send, "tp", bit)
        if late and 2 * bit >= size:
            other = after(other, *late)
        held = [
            jnp.where(low, a, b) + other[slot].astype(F32)
            for slot, (a, b) in enumerate(zip(held[0::2], held[1::2]))
        ]
        bit *= 2
    return held[0]


def queue_gather(part):
    return lax.all_gather(part, "tp", axis=1, tiled=True)


def queue_scatter_sum(partial):
    return lax.psum_scatter(partial.astype(BF16), "tp", scatter_dimension=1, tiled=True)


def owner_order(array):
    size = lax.axis_size("fsdp")
    index = lax.axis_index("fsdp")
    width = array.shape[1] // size
    cut = lambda owner: lax.dynamic_slice_in_dim(array, owner * width, width, 1)
    away = jnp.concatenate([cut(index ^ 1 ^ (2 * m)) for m in range(size // 2)], 1)
    return lax.optimization_barrier([away] + [cut(index ^ (2 * m)) for m in range(size // 2)])


def owner_terms(blocks, terms_of, axis):
    away = terms_of(blocks[0]).astype(BF16)
    other = exchange(away, "fsdp", 1)
    width = away.shape[axis] // (len(blocks) - 1)
    terms, sent = [], []
    for m, block in enumerate(blocks[1:]):
        share = lax.slice_in_dim(other, m * width, (m + 1) * width, axis=axis)
        term = terms_of(block) + share.astype(F32)
        if m:
            sent.append(term.astype(BF16))
        if m:
            term = exchange(sent[-1], "fsdp", 2 * m)
        terms.append(term)
    return terms, sent


def owner_total(terms, *earlier):
    terms = lax.optimization_barrier(tuple(terms) + earlier)[: len(terms)]
    return sum(term.astype(F32) for term in terms)


def after(value, *earlier):
    return lax.optimization_barrier((value,) + earlier)[0]


def allowed_keys(offsets, row_count, back):
    row = jnp.arange(row_count, dtype=jnp.int32)[:, None] + back * row_count
    first = row - offsets[..., None]
    key = jnp.arange((back + 1) * row_count, dtype=jnp.int32)[None, :]
    return ((key >= first) & (key <= row))[:, None]


def attend_forward(query_rotated, keys, values, allowed, score_scale):
    scores = (
        jnp.einsum("blhd,bmd->bhlm", query_rotated, keys, preferred_element_type=F32)
        * score_scale
    )
    scores = jnp.where(allowed, scores, MASKED_SCORE)
    row_max = jnp.max(scores, -1)
    row_sum = jnp.sum(jnp.where(allowed, jnp.exp(scores - row_max[..., None]), 0.0), -1)
    log_total = row_max + jnp.log(row_sum)
    prob_round = jnp.where(allowed, jnp.exp(scores - log_total[..., None]), 0.0).astype(BF16)
    heads = jnp.einsum("bhlm,bmd->blhd", prob_round, values, preferred_element_type=F32)
    return (heads.astype(BF16), log_total)


def attention_weights(query_rotated, keys, allowed, log_total, score_scale):
    scores = (
        jnp.einsum("blhd,bmd->bhlm", query_rotated, keys, preferred_element_type=F32)
        * score_scale
    )
    weights = jnp.where(allowed, jnp.exp(scores - log_total[..., None]), 0.0).astype(BF16)
    return lax.optimization_barrier(weights)


def attend_backward(query_rotated, keys, values, weights, heads_low, grad_low, score_scale):
    delta = jnp.swapaxes(jnp.sum(grad_low.astype(F32) * heads_low.astype(F32), -1), 1, 2)
    grad_values = jnp.einsum("bhlm,blhd->bmd", weights, grad_low, preferred_element_type=F32)
    grad_probs = jnp.einsum("blhd,bmd->bhlm", grad_low, values, preferred_element_type=F32)
    grad_scores = (
        weights.astype(F32) * (grad_probs - delta[..., None]) * score_scale
    ).astype(BF16)
    grad_query = jnp.einsum("bhlm,bmd->blhd", grad_scores, keys, preferred_element_type=F32)
    grad_keys = jnp.einsum(
        "bhlm,blhd->bmd", grad_scores, query_rotated, preferred_element_type=F32
    )
    return (grad_query, grad_keys, grad_values)


def shards(
    tokens,
    out_grad,
    segment_ids,
    positions,
    attn_norm,
    w_query,
    key_projection_weight,
    value_projection_weight,
    w_out,
    mlp_norm,
    w_gate,
    w_up,
    w_down,
):
    batch_count, row_count, local_width = tokens.shape
    full_width = local_width * lax.axis_size("tp")
    group_size = SEQUENCE_LENGTH // row_count
    stride = lax.axis_size("fsdp") // group_size
    query_width = w_query.shape[1]
    hidden = w_gate.shape[1]
    head_count = query_width // HEAD_SIZE
    score_scale = HEAD_SIZE ** (-0.5)
    back = min(group_size - 1, -(-(DOC_MAX - 1) // row_count))
    column_start = lax.axis_index("tp") * local_width
    shard_rows = w_query.shape[0]

    gains = jnp.stack([attn_norm, mlp_norm], 1)
    gains = jnp.pad(gains, ((0, 0), (0, GAIN_COLUMNS - 2)))
    first_shard = jnp.concatenate(
        [w_query, key_projection_weight, value_projection_weight, gains], 1
    )
    project_width = query_width + 2 * HEAD_SIZE
    first_full = lax.all_gather(first_shard, "fsdp", axis=0, tiled=True)
    project_weight = first_full[:, :project_width]
    gain_rows = first_full[:, project_width : project_width + 2].astype(F32).T
    gain_one, gain_two = gain_rows[0], gain_rows[1]
    rows = batch_count * row_count
    tokens_own = tokens.reshape(rows, local_width)
    gate_up_shard = lax.optimization_barrier(jnp.concatenate([w_gate, w_up], 1))
    tables, allowed, gain_one, gain_two = lax.optimization_barrier(
        (
            rope_tables(positions.reshape(rows), HEAD_SIZE),
            allowed_keys(positions, row_count, back),
            gain_one,
            gain_two,
        )
    )
    tokens_full = tp_gather(tokens_own, gate_up_shard, gain_one)
    out_weight = lax.all_gather(after(w_out, tokens_full), "fsdp", axis=1, tiled=True)
    gate_up_weight = lax.all_gather(
        after(gate_up_shard, tokens_full), "fsdp", axis=0, tiled=True
    )
    down_weight = lax.all_gather(after(w_down, tokens_full), "fsdp", axis=1, tiled=True)

    by_batch = lambda array: array.reshape((batch_count, row_count) + array.shape[1:])
    all_rows = lambda array: array.reshape((rows,) + array.shape[2:])
    inputs = tokens_full.astype(F32)
    scale_one = lax.rsqrt(jnp.mean(inputs * inputs, -1, keepdims=True) + NORM_EPSILON)
    normed_one = (inputs * scale_one * gain_one).astype(BF16)
    projected = dot_nn(normed_one, project_weight)
    query_rotated = by_batch(
        apply_rotary(
            projected[:, :query_width].reshape(rows, head_count, HEAD_SIZE), *tables
        ).astype(BF16)
    )
    key_rotated = apply_rotary(
        projected[:, None, query_width : query_width + HEAD_SIZE], *tables
    )[:, 0].astype(BF16)
    pairs = by_batch(
        jnp.concatenate([key_rotated, projected[:, query_width + HEAD_SIZE :].astype(BF16)], -1)
    )
    grad_in = tp_gather_far(after(out_grad.reshape(rows, local_width), tokens_full), pairs)
    window = [passed_along(pairs, "fsdp", o * stride) for o in range(back, 0, -1)]
    window = jnp.concatenate(window + [pairs], 1)
    keys, values = window[..., :HEAD_SIZE], window[..., HEAD_SIZE:]
    heads, totals = attend_forward(query_rotated, keys, values, allowed, score_scale)
    heads_out = heads.reshape(rows, query_width)
    middle_own = tokens_own.astype(F32) + tp_scatter_sum(
        dot_nn(after(heads_out, grad_in), out_weight)
    )
    middle = tp_gather(middle_own.astype(BF16)).astype(F32)

    scale_two = lax.rsqrt(jnp.mean(middle * middle, -1, keepdims=True) + NORM_EPSILON)
    normed_two = lax.optimization_barrier((middle * scale_two * gain_two).astype(BF16))
    both = dot_nn(normed_two, gate_up_weight)
    gate, up_proj = both[:, :hidden], both[:, hidden:]
    sigmoid_gate = jax.nn.sigmoid(gate)
    activated = (gate * sigmoid_gate * up_proj).astype(BF16)
    grad_act = dot_nn(grad_in, down_weight.T)
    grad_gate_low = (
        grad_act * up_proj * sigmoid_gate * (1.0 + gate * (1.0 - sigmoid_gate))
    ).astype(BF16)
    grad_up_low = (grad_act * gate * sigmoid_gate).astype(BF16)
    partial_two = queue_scatter_sum(
        dot_nt(grad_gate_low, gate_up_weight[:, :hidden])
        + dot_nt(grad_up_low, gate_up_weight[:, hidden:])
    )
    normed_two_order = owner_order(normed_two)
    gate_terms, gate_sent = owner_terms(
        normed_two_order, lambda block: dot_tn(block, grad_gate_low), 0
    )
    up_terms, up_sent = owner_terms(normed_two_order, lambda block: dot_tn(block, grad_up_low), 0)
    grads_order = owner_order(grad_in)
    down_terms, _ = owner_terms(grads_order, lambda block: dot_tn(activated, block), 1)
    grad_normed_two = queue_gather(after(partial_two, *gate_sent, *up_sent))
    weights = attention_weights(
        after(query_rotated, grad_up_low), keys, allowed, totals, score_scale
    )
    mlp_partial = dot_nn(activated, down_weight).astype(BF16)
    mlp_own = queue_scatter_sum(after(mlp_partial, grad_normed_two))
    output = (middle_own + mlp_own.astype(F32)).astype(BF16)

    gain_one_own = lax.dynamic_slice_in_dim(gain_one, column_start, local_width, 0)
    grad_two = grad_normed_two.astype(F32)
    norm_sum_two = jnp.sum(grad_two * middle * scale_two, 0)
    scaled_two = grad_two * gain_two
    grad_middle = (
        grad_in.astype(F32)
        + scale_two * scaled_two
        - middle
        * (scale_two * scale_two * scale_two)
        * jnp.mean(scaled_two * middle, -1, keepdims=True)
    )
    middle_low = lax.optimization_barrier(grad_middle.astype(BF16))
    grad_heads = by_batch(
        dot_nt(middle_low, out_weight).astype(BF16).reshape(rows, head_count, HEAD_SIZE)
    )
    grad_query_rot, grad_keys, grad_values = attend_backward(
        query_rotated, keys, values, weights, heads, grad_heads, score_scale
    )
    grad_window = jnp.concatenate([grad_keys, grad_values], -1)
    own_pairs = grad_window[:, back * row_count :]
    for o in range(1, back + 1):
        block = grad_window[:, (back - o) * row_count : (back - o + 1) * row_count]
        own_pairs = own_pairs + passed_along(block.astype(BF16), "fsdp", -o * stride).astype(F32)
    own_pairs = all_rows(own_pairs)
    grad_query_low = (
        reverse_rotary(all_rows(grad_query_rot), *tables).reshape(rows, query_width).astype(BF16)
    )
    grad_key_low = reverse_rotary(own_pairs[:, None, :HEAD_SIZE], *tables)[:, 0].astype(BF16)
    grad_value_low = own_pairs[:, HEAD_SIZE:].astype(BF16)
    grad_projected = lax.optimization_barrier(
        jnp.concatenate([grad_query_low, grad_key_low, grad_value_low], 1)
    )
    normed_one_order = owner_order(normed_one)
    project_terms, project_sent = owner_terms(
        normed_one_order, lambda block: dot_tn(block, grad_projected), 0
    )
    grad_one = dot_nt(grad_projected, project_weight)
    weighted = grad_one * inputs
    norm_sum_one = jnp.sum(weighted * scale_one, 0)
    summed = queue_scatter_sum(after(grad_one.astype(BF16), mlp_own)).astype(F32)
    small = jnp.concatenate([norm_sum_one, jnp.sum(weighted * gain_one, -1) / full_width])
    for bit in range((lax.axis_size("tp") - 1).bit_length()):
        small = small + exchange(small, "tp", 1 << bit)
    row_mean = small[full_width:, None]
    norm_sums = jnp.concatenate([small[:full_width], norm_sum_two])
    for bit in range((lax.axis_size("fsdp") - 1).bit_length()):
        norm_sums = norm_sums + exchange(norm_sums, "fsdp", 1 << bit)
    grad_middle_own = lax.dynamic_slice_in_dim(grad_middle, column_start, local_width, 1)
    input_grad = (
        grad_middle_own
        + scale_one * (summed * gain_one_own)
        - tokens_own.astype(F32) * (scale_one * scale_one * scale_one) * row_mean
    )
    middle_order = owner_order(after(middle_low, *project_sent))
    out_terms, out_sent = owner_terms(middle_order, lambda block: dot_tn(heads_out, block), 1)
    grad_scale = (batch_count * row_count * lax.axis_size("fsdp")) ** (-0.5)
    norm_start = lax.axis_index("fsdp") * shard_rows
    norm_sums = norm_sums * grad_scale
    down_sum = owner_total(down_terms, *out_sent)
    gate_sum = owner_total(gate_terms, *out_sent)
    up_sum = owner_total(up_terms, *out_sent)
    out_sum = owner_total(out_terms)
    project_sum = owner_total(project_terms, *out_sent) * grad_scale
    return (
        by_batch(output),
        by_batch(input_grad),
        lax.dynamic_slice_in_dim(norm_sums, norm_start, shard_rows, 0),
        project_sum[:, :query_width],
        project_sum[:, query_width : query_width + HEAD_SIZE],
        project_sum[:, query_width + HEAD_SIZE :],
        out_sum * grad_scale,
        lax.dynamic_slice_in_dim(norm_sums, full_width + norm_start, shard_rows, 0),
        gate_sum * grad_scale,
        up_sum * grad_scale,
        down_sum * grad_scale,
    )


def solution(mesh):
    in_specs = (
        P(None, "fsdp", "tp"),
        P(None, "fsdp", "tp"),
        P(None, "fsdp"),
        P(None, "fsdp"),
        P("fsdp"),
        P("fsdp", "tp"),
        P("fsdp", "tp"),
        P("fsdp", "tp"),
        P("tp", "fsdp"),
        P("fsdp"),
        P("fsdp", "tp"),
        P("fsdp", "tp"),
        P("tp", "fsdp"),
    )
    out_specs = (
        P(None, "fsdp", "tp"),
        P(None, "fsdp", "tp"),
        P("fsdp"),
        P("fsdp", "tp"),
        P("fsdp", "tp"),
        P("fsdp", "tp"),
        P("tp", "fsdp"),
        P("fsdp"),
        P("fsdp", "tp"),
        P("fsdp", "tp"),
        P("tp", "fsdp"),
    )

    return jax.shard_map(shards, mesh=mesh, in_specs=in_specs, out_specs=out_specs, check_vma=False)
```
